32 devices in a mesh: seq: 16 (over z, x, core), tp: 2 (over y).
Axes of the slice: x: 2, y: 2, z: 4, core: 2. Of those that a mesh axis runs over, the one named last changes fastest.
Arguments:
- tokens: bfloat16 [256, 8192], P('tp', 'seq'), may hold values from -6 to 6
- gate_weight: bfloat16 [8192, 14336], P('seq', 'tp'), may hold values from -0.0625 to 0.0625
- up_weight: bfloat16 [8192, 14336], P('seq', 'tp'), may hold values from -0.0625 to 0.0625
- down_weight: bfloat16 [14336, 8192], P('tp', 'seq'), may hold values from -0.09375 to 0.09375
- masks: int32 [2, 112], P(None, 'tp'), may hold values from 0 to 1, as said below
- cotangent: bfloat16 [256, 8192], P('tp', 'seq'), may hold values from -6 to 6
Outputs:
- output: bfloat16 [256, 8192], P('tp', 'seq')
- grad_tokens: bfloat16 [256, 8192], P('tp', 'seq')
- grad_gate: float32 [8192, 14336], P('seq', 'tp')
- grad_up: float32 [8192, 14336], P('seq', 'tp')
- grad_down: float32 [14336, 8192], P('tp', 'seq')
The draws below stay inside these ranges and needn't reach their ends.
Inputs may be any that keep to these rules, and one draw needn't show every extreme that they name: Each row of masks holds exactly 28 ones. Cut a row into 2 groups of 56 consecutive blocks: in every row one group holds exactly 28 ones, and the remaining ones are spread over the other groups as evenly as possible, so that their counts differ by at most one.
All inputs are finite; a program needn't handle non-finite values.
Results may differ from the reference program's by a relative error of at most 0.0049.
Values may be sent and summed in bfloat16 or wider, within the bound.
A program may use at most 192 MiB of HBM per device.

```python
import math
import jax
import jax.numpy as jnp

D = 8192
FF = 14336
BLK = 128
ROWBLK = 128
SEQUENCE_TOKENS = 256
KEEP = 28
N_TP = 2


def draw_masks(key, part):
    block_total = FF // BLK
    kept_total = block_total // 4
    row_blocks = SEQUENCE_TOKENS // ROWBLK
    per_shard = block_total // N_TP
    capacity = 2 * kept_total // N_TP
    remainder = kept_total - capacity
    base_count = remainder // (N_TP - 1)
    extra_count = remainder % (N_TP - 1)

    def one_row(row_key):
        perm_key, selection_key = jax.random.split(row_key)
        order = jax.random.permutation(perm_key, N_TP)
        position = jnp.argsort(order, stable=True).astype(jnp.int32)
        shard_count = jnp.where(position == 0, capacity, base_count + (position - 1 < extra_count).astype(jnp.int32))
        block_rank = jax.vmap(lambda inner_key: jax.random.permutation(inner_key, per_shard))(jax.random.split(selection_key, N_TP))
        chosen = (block_rank < shard_count[:, None]).astype(jnp.int32)
        return chosen.reshape(block_total)
    return jax.vmap(one_row)(jax.random.split(key, row_blocks)).astype(jnp.int32)


def level_of(rng, extent, cuts, least, top_value):
    def one(axis_at, blocks):
        draws = jax.random.uniform(jax.random.fold_in(jax.random.fold_in(rng, 6), axis_at), (blocks,), jnp.float32, least / len(cuts), top_value / len(cuts))
        return jnp.repeat(jnp.exp(draws), extent[axis_at] // blocks).reshape((-1,) + (1,) * (len(extent) - axis_at - 1))

    loudness = one(*cuts[0])
    for cut in cuts[1:]:
        loudness = loudness * one(*cut)
    return loudness


def normal_values(own_key, shape, scale, limit, cuts=(), held_as=jnp.bfloat16):
    drawn = jax.random.normal(own_key, shape, jnp.float32) * scale
    if len(cuts) > 0:
        drawn = level_of(own_key, shape, cuts, -0.22, 0.18) * drawn
    return jnp.clip(drawn, min=-limit, max=limit).astype(held_as)


def setup_inputs(seed: int = 0) -> dict:
    key_of = jax.random.split(jax.random.key(seed), 7)
    tokens = normal_values(key_of[0], (SEQUENCE_TOKENS, D), 1.0, 6.0, ((0, 2), (1, 16)))
    gate_weight = normal_values(key_of[1], (D, FF), D ** -0.5, 0.0625, ((0, 16), (1, 2)))
    up_weight = normal_values(key_of[2], (D, FF), D ** -0.5, 0.0625, ((0, 16), (1, 2)))
    down_weight = normal_values(key_of[3], (FF, D), (KEEP * BLK) ** -0.5, 0.09375, ((0, 2), (1, 16)))
    masks = draw_masks(jax.random.fold_in(key_of[6], 71), 0)
    cotangent = normal_values(key_of[5], (SEQUENCE_TOKENS, D), 1.0, 6.0, ((0, 2), (1, 16)))
    return {"tokens": tokens, "gate_weight": gate_weight, "up_weight": up_weight, "down_weight": down_weight, "masks": masks, "cotangent": cotangent}


def reference(tokens, gate_weight, up_weight, down_weight, masks, cotangent):
    keep = jnp.repeat(jnp.repeat(masks, ROWBLK, axis=0), BLK, axis=1).astype(jnp.float32)
    gate = jnp.dot(tokens, gate_weight, preferred_element_type=jnp.float32)
    up = jnp.dot(tokens, up_weight, preferred_element_type=jnp.float32)
    hidden = (jax.nn.silu(gate) * up * keep).astype(jnp.bfloat16)
    output = jnp.dot(hidden, down_weight, preferred_element_type=jnp.float32).astype(jnp.bfloat16)
    grad_hidden = jnp.dot(cotangent, down_weight.T, preferred_element_type=jnp.float32) * keep
    sigmoid_gate = jax.nn.sigmoid(gate)
    grad_gate_act = (grad_hidden * up * sigmoid_gate * (1.0 + gate * (1.0 - sigmoid_gate))).astype(jnp.bfloat16)
    grad_up_act = (grad_hidden * gate * sigmoid_gate).astype(jnp.bfloat16)
    grad_scale = 1.0 / math.sqrt(SEQUENCE_TOKENS)
    grad_gate = jnp.dot(tokens.T, grad_gate_act, preferred_element_type=jnp.float32) * grad_scale
    grad_up = jnp.dot(tokens.T, grad_up_act, preferred_element_type=jnp.float32) * grad_scale
    grad_down = jnp.dot(hidden.T, cotangent, preferred_element_type=jnp.float32) * grad_scale
    grad_tokens = (jnp.dot(grad_gate_act, gate_weight.T, preferred_element_type=jnp.float32) + jnp.dot(grad_up_act, up_weight.T, preferred_element_type=jnp.float32)).astype(jnp.bfloat16)
    return (output, grad_tokens, grad_gate, grad_up, grad_down)
```

```python
import functools
import math

import jax
import jax.numpy as jnp
from jax import lax
from jax.experimental import pallas as pl
from jax.experimental.pallas import tpu as pltpu
from jax.sharding import PartitionSpec as P

BLK = 128
ROWBLK = 128
KEEP_PART = 4
MESH = pl.DeviceIdType.MESH
PLAIN_LIMIT = 40 * 1024 * 1024
COMM_LIMIT = 48 * 1024 * 1024


def group_of(count):
    for size in (7, 8, 4, 2):
        if count % size == 0:
            return size
    return 1


def tables_kernel(first_ref, mask_ref, block_ref, live_ref, slot_ref):
    row_blocks, capacity = block_ref.shape
    blocks = mask_ref.shape[1]
    for row in range(row_blocks):
        source = first_ref[0] + row
        for slot in range(capacity):
            block_ref[row, slot] = 0
            live_ref[row, slot] = 0

        def step(block, taken, row=row, source=source):
            kept = mask_ref[source, block]
            at = jnp.minimum(taken, capacity - 1)
            slot_ref[row, block] = jnp.where(kept == 1, row * capacity + at, -1)

            @pl.when(kept == 1)
            def _():
                block_ref[row, at] = block
                live_ref[row, at] = 1

            return taken + kept

        lax.fori_loop(0, blocks, step, jnp.int32(0))


def slot_tables(masks, first, row_blocks, capacity):
    blocks = masks.shape[1]
    smem = pl.BlockSpec(memory_space=pltpu.SMEM)
    return pl.pallas_call(
        tables_kernel,
        out_shape=(
            jax.ShapeDtypeStruct((row_blocks, capacity), jnp.int32),
            jax.ShapeDtypeStruct((row_blocks, capacity), jnp.int32),
            jax.ShapeDtypeStruct((row_blocks, blocks), jnp.int32),
        ),
        in_specs=[smem, smem],
        out_specs=(smem, smem, smem),
    )(first.reshape(1), masks)


def rows_kernel(count, tok_ref, cot_ref, tok_all, cot_all, send_sem, recv_sem, own_sem):
    me = lax.axis_index("tp")
    barrier = pltpu.get_barrier_semaphore()
    for shift in range(1, count):
        pl.semaphore_signal(
            barrier, inc=1, device_id={"tp": lax.rem(me + shift, count)}, device_id_type=MESH
        )
    pl.semaphore_wait(barrier, count - 1)
    copies = []
    for which, (src, dst) in enumerate(((tok_ref, tok_all), (cot_ref, cot_all))):
        for shift in range(1, count):
            copy = pltpu.make_async_remote_copy(
                src_ref=src,
                dst_ref=dst.at[me],
                send_sem=send_sem.at[which, shift],
                recv_sem=recv_sem.at[which, shift],
                device_id={"tp": lax.rem(me + shift, count)},
                device_id_type=MESH,
            )
            copy.start()
            copies.append(copy)
        own = pltpu.make_async_copy(src, dst.at[me], own_sem.at[which])
        own.start()
        copies.append(own)
    for copy in copies:
        copy.wait()


def gather_rows(tokens, cotangent):
    count = lax.axis_size("tp")
    rows, feats = tokens.shape
    anywhere = pl.BlockSpec(memory_space=pl.ANY)
    return pl.pallas_call(
        functools.partial(rows_kernel, count),
        out_shape=(jax.ShapeDtypeStruct((count, rows, feats), tokens.dtype),) * 2,
        in_specs=[anywhere] * 2,
        out_specs=(anywhere,) * 2,
        scratch_shapes=[
            pltpu.SemaphoreType.DMA((2, count)),
            pltpu.SemaphoreType.DMA((2, count)),
            pltpu.SemaphoreType.DMA((2,)),
        ],
        compiler_params=pltpu.CompilerParams(collective_id=0, has_side_effects=True),
    )(tokens, cotangent)


def parts_kernel(group, block_ref, live_ref, tok_ref, cot_ref, *refs):
    gates, ups, downs = refs[:group], refs[group : 2 * group], refs[2 * group : 3 * group]
    out_ref = refs[3 * group]
    row, step = pl.program_id(0), pl.program_id(1)
    tok, cot = tok_ref[...], cot_ref[...]
    for at in range(group):
        live = live_ref[row, step * group + at] == 1
        rows = slice(at * ROWBLK, (at + 1) * ROWBLK)
        both = jnp.dot(
            tok,
            jnp.concatenate([gates[at][...], ups[at][...]], axis=1),
            preferred_element_type=jnp.float32,
        )
        grad = lax.dot_general(
            cot, downs[at][...], (((1,), (1,)), ((), ())), preferred_element_type=jnp.float32
        )
        out_ref[0, rows, :] = both[:, :BLK]
        out_ref[1, rows, :] = jnp.where(live, both[:, BLK:], 0.0)
        out_ref[2, rows, :] = jnp.where(live, grad, 0.0)


def weight_specs(group, feats):
    def columns(at):
        return pl.BlockSpec(
            (feats, BLK), lambda row, step, block, live: (0, block[row, step * group + at])
        )

    def rows(at):
        return pl.BlockSpec(
            (BLK, feats), lambda row, step, block, live: (block[row, step * group + at], 0)
        )

    return (
        [columns(at) for at in range(group)] * 2 + [rows(at) for at in range(group)]
    )


def partial_products(block, live, tok, cot, gate_w, up_w, down_w):
    row_blocks, capacity = block.shape
    feats = tok.shape[1]
    group = group_of(capacity)
    steps = capacity // group
    rows_spec = pl.BlockSpec((ROWBLK, feats), lambda row, step, block, live: (row, 0))
    flops = 6 * row_blocks * ROWBLK * feats * capacity * BLK
    return pl.pallas_call(
        functools.partial(parts_kernel, group),
        out_shape=jax.ShapeDtypeStruct((3, row_blocks * capacity * ROWBLK, BLK), jnp.float32),
        grid_spec=pltpu.PrefetchScalarGridSpec(
            num_scalar_prefetch=2,
            grid=(row_blocks, steps),
            in_specs=[rows_spec, rows_spec] + weight_specs(group, feats),
            out_specs=pl.BlockSpec(
                (3, group * ROWBLK, BLK), lambda row, step, block, live: (0, row * steps + step, 0)
            ),
        ),
        compiler_params=pltpu.CompilerParams(vmem_limit_bytes=PLAIN_LIMIT),
        cost_estimate=pl.CostEstimate(
            flops=flops, bytes_accessed=flops // ROWBLK, transcendentals=0
        ),
    )(block, live, tok, cot, *([gate_w] * group + [up_w] * group + [down_w] * group))


def exchange_kernel(
    count, part_ref, all_ref, paired, xsend, xland, zsend, zland, acts,
    pair_send, pair_recv, x_send, x_recv, z_send, z_recv,
    up_send, down_send, side_send, all_recv, hand_send, hand_recv, own_sem,
):
    _, _, halves, wide, tall, _, _ = part_ref.shape
    chips = count // 2
    me = lax.axis_index("seq")
    chip, core = me // 2, lax.rem(me, 2)
    sibling = {"seq": me + 1 - 2 * core}
    along, across = chip // wide, lax.rem(chip, wide)
    order = sorted(range(1, tall), key=lambda shift: abs(2 * shift - tall))

    def device(i, j):
        return {"seq": (i * wide + j) * 2 + core}

    def column(shift):
        return lax.rem(across + shift, wide)

    def line(shift):
        return lax.rem(along + shift, tall)

    def remote(src, dst, send, recv, target):
        return pltpu.make_async_remote_copy(
            src_ref=src, dst_ref=dst, send_sem=send, recv_sem=recv,
            device_id=target, device_id_type=MESH,
        )

    barrier = pltpu.get_barrier_semaphore()
    pl.semaphore_signal(barrier, inc=1, device_id=sibling, device_id_type=MESH)
    for s in range(1, wide):
        pl.semaphore_signal(
            barrier, inc=1, device_id=device(along, column(s)), device_id_type=MESH
        )
    for d in range(1, tall):
        pl.semaphore_signal(barrier, inc=1, device_id=device(line(d), across), device_id_type=MESH)
    pl.semaphore_wait(barrier, wide + tall - 1)

    def pair_copy(h, s, d):
        return remote(
            part_ref.at[:, 1 - core, h, column(s), line(d)], paired.at[h, s, d],
            pair_send.at[h, s, d], pair_recv.at[h, s, d], sibling,
        )

    def x_copy(h, s, d):
        return remote(
            xsend.at[h, s - 1, d], xland.at[h, s - 1, d],
            x_send.at[h, s, d], x_recv.at[h, s, d], device(along, column(s)),
        )

    def z_copy(h, d):
        return remote(
            zsend.at[h, d - 1], zland.at[h, d - 1],
            z_send.at[h, d], z_recv.at[h, d], device(line(d), across),
        )

    def slot(h, i, j, side):
        return all_ref.at[:, side, h, j, i]

    def z_route(h, i, j, to, send, src=None):
        dst = slot(h, i, j, core)
        owner = i * wide + j
        return remote(
            dst if src is None else src, dst, send.at[h, owner], all_recv.at[h, owner],
            device(to, across),
        )

    def x_route(h, i, s, src=None):
        dst = slot(h, i, across, core)
        return remote(
            dst if src is None else src, dst, side_send.at[h, s, i],
            all_recv.at[h, i * wide + across], device(along, column(s)),
        )

    def hand_copy(h, i, j, side, src=None):
        dst = slot(h, i, j, side)
        owner = i * wide + j
        return remote(
            dst if src is None else src, dst, hand_send.at[h, owner], hand_recv.at[h, owner], sibling
        )

    def take(h, i, j):
        z_route(h, i, j, along, up_send).wait_recv()

    def pass_on(h, i, j, up, down, src=None):
        if up:

            @pl.when(along < tall - 1)
            def _():
                z_route(h, i, j, along + 1, up_send, src).start()

        if down:

            @pl.when(along > 0)
            def _():
                z_route(h, i, j, along - 1, down_send, src).start()

    def spread(h, i, src=None):
        for s in range(1, wide):
            x_route(h, i, s, src).start()

    for h in range(halves):
        for s in list(range(1, wide)) + [0]:
            for d in order + [0]:
                pair_copy(h, s, d).start()

    for h in range(halves):
        for d in order + [0]:
            for s in range(1, wide):
                pair_copy(h, s, d).wait_recv()
                xsend[h, s - 1, d] = (
                    part_ref[:, core, h, column(s), line(d)] + paired[h, s, d]
                ).astype(jnp.bfloat16)
                x_copy(h, s, d).start()

    def row_sum(h, d):
        pair_copy(h, 0, d).wait_recv()
        total = part_ref[:, core, h, across, line(d)] + paired[h, 0, d]
        for s in range(1, wide):
            x_copy(h, s, d).wait_recv()
            total = total + xland[h, s - 1, d].astype(jnp.float32)
        return total

    for h in range(halves):
        for d in order:
            zsend[h, d - 1] = row_sum(h, d).astype(jnp.bfloat16)
            z_copy(h, d).start()

    def own_copy(h):
        return pltpu.make_async_copy(acts.at[h], slot(h, along, across, core), own_sem.at[h])

    for h in range(halves):
        total = row_sum(h, 0)
        for d in order:
            z_copy(h, d).wait_recv()
            total = total + zland[h, d - 1].astype(jnp.float32)
        gate, up, grad = total[0], total[1], total[2]
        sig = jax.nn.sigmoid(gate)
        acts[h, 0] = (gate * sig * up).astype(jnp.bfloat16)
        acts[h, 1] = (grad * up * sig * (1.0 + gate * (1.0 - sig))).astype(jnp.bfloat16)
        acts[h, 2] = (grad * gate * sig).astype(jnp.bfloat16)
        src = acts.at[h]
        pass_on(h, along, across, True, True, src)
        spread(h, along, src)
        hand_copy(h, along, across, core, src).start()
        own_copy(h).start()

    for h in range(halves):
        if h % 2 == 1:
            for s in range(1, wide):
                take(h, along, column(s))
                pass_on(h, along, column(s), True, True)
                hand_copy(h, along, column(s), core).start()
    for far in range(1, tall):
        for h in range(halves):
            for s in range(wide if h % 2 == 1 else 1):
                for sign in (-1, 1):

                    @pl.when(along >= far if sign < 0 else along + far < tall)
                    def _(h=h, s=s, sign=sign):
                        i = along + sign * far
                        take(h, i, column(s))
                        pass_on(h, i, column(s), sign < 0, sign > 0)
                        if h % 2 == 0:
                            spread(h, i)
                        hand_copy(h, i, column(s), core).start()

    for h in range(0, halves, 2):
        for s in range(1, wide):
            for d in [0] + list(range(1, tall)):
                take(h, line(d), column(s))
                hand_copy(h, line(d), column(s), core).start()

    for h in range(halves):
        own_copy(h).wait()

        def finish(owner, carry, h=h):
            i, j = owner // wide, lax.rem(owner, wide)
            hand_copy(h, i, j, 1 - core).wait_recv()
            hand_copy(h, i, j, core).wait_send()
            mine = jnp.bool_(True) if h % 2 == 1 else j == across

            @pl.when(jnp.logical_and(mine, jnp.logical_and(i <= along, along < tall - 1)))
            def _():
                z_route(h, i, j, along + 1, up_send).wait_send()

            @pl.when(jnp.logical_and(mine, jnp.logical_and(i >= along, along > 0)))
            def _():
                z_route(h, i, j, along - 1, down_send).wait_send()

            return carry

        lax.fori_loop(0, chips, finish, 0)
        for s in range(1, wide):
            if h % 2 == 1:
                x_route(h, along, s).wait_send()
            else:
                for i in range(tall):
                    x_route(h, i, s).wait_send()
        for d in range(tall):
            for s in range(wide):
                pair_copy(h, s, d).wait_send()
                if s > 0:
                    x_copy(h, s, d).wait_send()
            if d > 0:
                z_copy(h, d).wait_send()


def exchange(parts, collective_id):
    count = lax.axis_size("seq")
    chips = count // 2
    tall = 4 if chips % 4 == 0 else chips
    wide = chips // tall
    own = parts.shape[1] // count
    halves = 2 if own % 32 == 0 else 1
    piece = own // halves
    shape = (3, 2, halves, wide, tall, piece, BLK)
    chunk = (3, piece, BLK)
    dma = pltpu.SemaphoreType.DMA
    out = pl.pallas_call(
        functools.partial(exchange_kernel, count),
        out_shape=jax.ShapeDtypeStruct(shape, jnp.bfloat16),
        in_specs=[pl.BlockSpec(memory_space=pltpu.VMEM)],
        out_specs=pl.BlockSpec(memory_space=pl.ANY),
        scratch_shapes=[
            pltpu.VMEM((halves, wide, tall) + chunk, jnp.float32),
            pltpu.VMEM((halves, max(wide - 1, 1), tall) + chunk, jnp.bfloat16),
            pltpu.VMEM((halves, max(wide - 1, 1), tall) + chunk, jnp.bfloat16),
            pltpu.VMEM((halves, max(tall - 1, 1)) + chunk, jnp.bfloat16),
            pltpu.VMEM((halves, max(tall - 1, 1)) + chunk, jnp.bfloat16),
            pltpu.VMEM((halves,) + chunk, jnp.bfloat16),
            dma((halves, wide, tall)),
            dma((halves, wide, tall)),
            dma((halves, wide, tall)),
            dma((halves, wide, tall)),
            dma((halves, tall)),
            dma((halves, tall)),
            dma((halves, chips)),
            dma((halves, chips)),
            dma((halves, wide, tall)),
            dma((halves, chips)),
            dma((halves, chips)),
            dma((halves, chips)),
            dma((halves,)),
        ],
        compiler_params=pltpu.CompilerParams(
            collective_id=collective_id, has_side_effects=True, vmem_limit_bytes=COMM_LIMIT
        ),
    )(parts.reshape(shape))
    return out.reshape(parts.shape)


def rows_out_kernel(group, block_ref, live_ref, act_ref, *refs):
    gates, ups, downs = refs[:group], refs[group : 2 * group], refs[2 * group : 3 * group]
    out_ref = refs[3 * group]
    step = pl.program_id(1)

    @pl.when(step == 0)
    def _():
        out_ref[...] = jnp.zeros_like(out_ref)

    out = jnp.zeros(out_ref.shape[2:], jnp.float32)
    grad = jnp.zeros(out_ref.shape[2:], jnp.float32)
    across = (((1,), (1,)), ((), ()))
    for at in range(group):
        rows = slice(at * ROWBLK, (at + 1) * ROWBLK)
        out += jnp.dot(act_ref[0, rows, :], downs[at][...], preferred_element_type=jnp.float32)
        grad += lax.dot_general(
            jnp.concatenate([act_ref[1, rows, :], act_ref[2, rows, :]], axis=1),
            jnp.concatenate([gates[at][...], ups[at][...]], axis=1),
            across,
            preferred_element_type=jnp.float32,
        )
    out_ref[0, 0] += out
    out_ref[0, 1] += grad


def rows_out(block, live, acts, gate_w, up_w, down_w):
    row_blocks, capacity = block.shape
    feats = gate_w.shape[0]
    group = group_of(capacity)
    steps = capacity // group
    flops = 6 * row_blocks * ROWBLK * feats * capacity * BLK
    return pl.pallas_call(
        functools.partial(rows_out_kernel, group),
        out_shape=jax.ShapeDtypeStruct((row_blocks, 2, ROWBLK, feats), jnp.float32),
        grid_spec=pltpu.PrefetchScalarGridSpec(
            num_scalar_prefetch=2,
            grid=(row_blocks, steps),
            in_specs=[
                pl.BlockSpec(
                    (3, group * ROWBLK, BLK),
                    lambda row, step, block, live: (0, row * steps + step, 0),
                )
            ]
            + weight_specs(group, feats),
            out_specs=pl.BlockSpec(
                (1, 2, ROWBLK, feats), lambda row, step, block, live: (row, 0, 0, 0)
            ),
        ),
        compiler_params=pltpu.CompilerParams(vmem_limit_bytes=PLAIN_LIMIT),
        cost_estimate=pl.CostEstimate(
            flops=flops, bytes_accessed=flops // ROWBLK, transcendentals=0
        ),
    )(block, live, acts, *([gate_w] * group + [up_w] * group + [down_w] * group))


def weights_out_kernel(
    group, scale, slot_ref, tok_ref, cot_ref, act_ref, gate_ref, up_ref, down_ref, flipped, dense
):
    step = pl.program_id(0)
    row_blocks = slot_ref.shape[0]

    @pl.when(step == 0)
    def _():
        flipped[...] = tok_ref[...].T

    for at in range(group):
        for row in range(row_blocks):
            unit = slot_ref[row, step * group + at]
            taken = pl.ds(pl.multiple_of(jnp.maximum(unit, 0) * ROWBLK, ROWBLK), ROWBLK)
            for which in range(3):
                value = act_ref[which, taken, :]
                dense[which, row * ROWBLK : (row + 1) * ROWBLK, at * BLK : (at + 1) * BLK] = (
                    jnp.where(unit >= 0, value, jnp.zeros_like(value))
                )
    tok = flipped[...]
    gate_ref[...] = jnp.dot(tok, dense[1], preferred_element_type=jnp.float32) * scale
    up_ref[...] = jnp.dot(tok, dense[2], preferred_element_type=jnp.float32) * scale
    down_ref[...] = (
        lax.dot_general(
            dense[0], cot_ref[...], (((0,), (0,)), ((), ())), preferred_element_type=jnp.float32
        )
        * scale
    )


def weights_out(slots, tok, cot, acts, scale):
    row_blocks, blocks = slots.shape
    rows, feats = tok.shape
    group = group_of(blocks)
    whole = pl.BlockSpec((rows, feats), lambda step, slot: (0, 0))
    wide = pl.BlockSpec((feats, group * BLK), lambda step, slot: (0, step))
    hidden = blocks * BLK
    return pl.pallas_call(
        functools.partial(weights_out_kernel, group, scale),
        out_shape=(
            jax.ShapeDtypeStruct((feats, hidden), jnp.float32),
            jax.ShapeDtypeStruct((feats, hidden), jnp.float32),
            jax.ShapeDtypeStruct((hidden, feats), jnp.float32),
        ),
        grid_spec=pltpu.PrefetchScalarGridSpec(
            num_scalar_prefetch=1,
            grid=(blocks // group,),
            in_specs=[
                whole,
                whole,
                pl.BlockSpec(acts.shape, lambda step, slot: (0, 0, 0)),
            ],
            out_specs=(
                wide,
                wide,
                pl.BlockSpec((group * BLK, feats), lambda step, slot: (step, 0)),
            ),
            scratch_shapes=[
                pltpu.VMEM((feats, rows), jnp.bfloat16),
                pltpu.VMEM((3, rows, group * BLK), jnp.bfloat16),
            ],
        ),
        compiler_params=pltpu.CompilerParams(vmem_limit_bytes=PLAIN_LIMIT),
        cost_estimate=pl.CostEstimate(
            flops=6 * rows * feats * hidden, bytes_accessed=12 * feats * hidden, transcendentals=0
        ),
    )(slots, tok, cot, acts)


def shards(tokens, gate_weight, up_weight, down_weight, masks, cotangent):
    tp_count = lax.axis_size("tp")
    rank = lax.axis_index("tp")
    rows, feats = tokens.shape
    total_rows = rows * tp_count
    row_blocks, blocks = masks.shape
    kept_total = blocks * tp_count // KEEP_PART
    capacity = min(2 * kept_total // tp_count, blocks)
    scale = 1.0 / math.sqrt(total_rows)
    weights = (gate_weight, up_weight, down_weight)
    swap = [(src, (src + 1) % tp_count) for src in range(tp_count)]

    def every_row(_):
        block, live, slots = slot_tables(masks, jnp.int32(0), row_blocks, capacity)
        tok, cot = (value.reshape(total_rows, feats) for value in gather_rows(tokens, cotangent))
        parts = partial_products(block, live, tok, cot, *weights)
        acts = exchange(parts, 1)
        row_parts = rows_out(block, live, acts, *weights)
        row_parts = jnp.swapaxes(row_parts.reshape(tp_count, rows // ROWBLK, 2, ROWBLK, feats), 1, 2)
        moved = []
        for shift in range(1, tp_count):
            piece = lax.dynamic_index_in_dim(
                row_parts, lax.rem(rank + shift, tp_count), 0, keepdims=False
            ).astype(jnp.bfloat16)
            pairs = [(src, (src + shift) % tp_count) for src in range(tp_count)]
            moved.append(lax.ppermute(piece, "tp", pairs))
        grads = weights_out(slots, tok, cot, acts, scale)
        mine = lax.dynamic_index_in_dim(row_parts, rank, 0, keepdims=False)
        for piece in moved:
            mine = mine + piece.astype(jnp.float32)
        mine = mine.reshape(2, rows, feats).astype(jnp.bfloat16)
        return (mine[0], mine[1]) + tuple(grads)

    if tp_count != 2 or row_blocks != 2 or rows != ROWBLK:
        return every_row(None)

    def one_row(own, _):
        tok, cot = tokens, cotangent
        if not own:
            tok, cot = lax.ppermute(tok, "tp", swap), lax.ppermute(cot, "tp", swap)
        first = rank if own else 1 - rank
        block, live, slots = slot_tables(masks, first, 1, capacity)
        parts = partial_products(block, live, tok, cot, *weights)
        acts = exchange(parts, 2 if own else 3)
        sums = rows_out(block, live, acts, *weights)[0].astype(jnp.bfloat16)
        if not own:
            sums = lax.ppermute(sums, "tp", swap)
        grads = weights_out(slots, tok, cot, acts, scale)
        return (sums[0], sums[1]) + tuple(grads)

    counts = jnp.sum(masks, axis=1)
    kept = counts > 0
    same = kept[0] == kept[1]
    case = jnp.where(same, 2, jnp.where(kept[0] == (rank == 0), 0, 1))
    return lax.switch(
        case,
        [functools.partial(one_row, True), functools.partial(one_row, False), every_row],
        None,
    )


def solution(mesh):
    placed = (
        P("tp", "seq"),
        P("seq", "tp"),
        P("seq", "tp"),
        P("tp", "seq"),
        P(None, "tp"),
        P("tp", "seq"),
    )
    return jax.shard_map(
        shards,
        mesh=mesh,
        in_specs=placed,
        out_specs=(P("tp", "seq"), P("tp", "seq"), P("seq", "tp"), P("seq", "tp"), P("tp", "seq")),
        check_vma=False,
    )
```

```python
import functools
import math

import jax
import jax.numpy as jnp
from jax import lax
from jax.experimental import pallas as pl
from jax.experimental.pallas import tpu as pltpu
from jax.sharding import PartitionSpec as P

BLK = 128
ROWBLK = 128
KEEP_PART = 4
MESH = pl.DeviceIdType.MESH
PLAIN_LIMIT = 20 * 1024 * 1024
COMM_LIMIT = 28 * 1024 * 1024
WIDE_LIMIT = 32 * 1024 * 1024


def group_of(count):
    for size in (7, 8, 4, 2):
        if count % size == 0:
            return size
    return 1


def tables_kernel(capacity, first_ref, mask_ref, table_ref, case_ref):
    row_blocks, blocks = mask_ref.shape
    counts = []
    for row in range(row_blocks):
        source = lax.rem(first_ref[0] + row, row_blocks)
        for slot in range(capacity + 1):
            table_ref[row, slot] = -1

        def step(block, taken, row=row, source=source):
            kept = mask_ref[source, block]
            at = jnp.minimum(taken, capacity)
            table_ref[row, at] = jnp.where(kept == 1, block, -1)
            table_ref[row, capacity + 1 + block] = jnp.where(kept == 1, at, -1)
            return taken + kept

        counts.append(lax.fori_loop(0, blocks, step, jnp.int32(0), unroll=8))
    mine, other = counts[0] > 0, counts[row_blocks - 1] > 0
    case_ref[0] = jnp.where(mine == other, 2, jnp.where(mine, 0, 1))


def unit_tables(masks, first, capacity):
    row_blocks, blocks = masks.shape
    smem = pl.BlockSpec(memory_space=pltpu.SMEM)
    return pl.pallas_call(
        functools.partial(tables_kernel, capacity),
        out_shape=(
            jax.ShapeDtypeStruct((row_blocks, capacity + 1 + blocks), jnp.int32),
            jax.ShapeDtypeStruct((1,), jnp.int32),
        ),
        in_specs=[smem, smem],
        out_specs=(smem, smem),
    )(first.reshape(1), masks)


def rows_kernel(count, tok_ref, cot_ref, tok_all, cot_all, send_sem, recv_sem, own_sem):
    me = lax.axis_index("tp")
    barrier = pltpu.get_barrier_semaphore()
    for shift in range(1, count):
        pl.semaphore_signal(
            barrier, inc=1, device_id={"tp": lax.rem(me + shift, count)}, device_id_type=MESH
        )
    pl.semaphore_wait(barrier, count - 1)
    copies = []
    for which, (src, dst) in enumerate(((tok_ref, tok_all), (cot_ref, cot_all))):
        for shift in range(1, count):
            copy = pltpu.make_async_remote_copy(
                src_ref=src,
                dst_ref=dst.at[me],
                send_sem=send_sem.at[which, shift],
                recv_sem=recv_sem.at[which, shift],
                device_id={"tp": lax.rem(me + shift, count)},
                device_id_type=MESH,
            )
            copy.start()
            copies.append(copy)
        own = pltpu.make_async_copy(src, dst.at[me], own_sem.at[which])
        own.start()
        copies.append(own)
    for copy in copies:
        copy.wait()


def gather_rows(tokens, cotangent):
    count = lax.axis_size("tp")
    rows, feats = tokens.shape
    anywhere = pl.BlockSpec(memory_space=pl.ANY)
    return pl.pallas_call(
        functools.partial(rows_kernel, count),
        out_shape=(jax.ShapeDtypeStruct((count, rows, feats), tokens.dtype),) * 2,
        in_specs=[anywhere] * 2,
        out_specs=(anywhere,) * 2,
        scratch_shapes=[
            pltpu.SemaphoreType.DMA((2, count)),
            pltpu.SemaphoreType.DMA((2, count)),
            pltpu.SemaphoreType.DMA((2,)),
        ],
        compiler_params=pltpu.CompilerParams(collective_id=0, has_side_effects=True),
    )(tokens, cotangent)


def parts_kernel(first, group, table_ref, tok_ref, cot_ref, *refs):
    gates, ups, downs = refs[:group], refs[group : 2 * group], refs[2 * group : 3 * group]
    out_ref = refs[3 * group]
    row, step = pl.program_id(0) + first, pl.program_id(1)
    tok, cot = tok_ref[...], cot_ref[...]
    for at in range(group):
        live = table_ref[row, step * group + at] >= 0
        rows = slice(at * ROWBLK, (at + 1) * ROWBLK)
        both = jnp.dot(
            tok,
            jnp.concatenate([gates[at][...], ups[at][...]], axis=1),
            preferred_element_type=jnp.float32,
        )
        grad = lax.dot_general(
            cot, downs[at][...], (((1,), (1,)), ((), ())), preferred_element_type=jnp.float32
        )
        out_ref[0, rows, :] = both[:, :BLK]
        out_ref[1, rows, :] = jnp.where(live, both[:, BLK:], 0.0)
        out_ref[2, rows, :] = jnp.where(live, grad, 0.0)


def weight_specs(first, group, feats):
    def block(table, row, step, at):
        return jnp.maximum(table[row + first, step * group + at], 0)

    def columns(at):
        return pl.BlockSpec((feats, BLK), lambda row, step, table: (0, block(table, row, step, at)))

    def rows(at):
        return pl.BlockSpec((BLK, feats), lambda row, step, table: (block(table, row, step, at), 0))

    return (
        [columns(at) for at in range(group)] * 2 + [rows(at) for at in range(group)]
    )


def partial_products(table, first, capacity, tok, cot, gate_w, up_w, down_w):
    row_blocks, feats = tok.shape[0] // ROWBLK, tok.shape[1]
    group = group_of(capacity)
    steps = capacity // group
    rows_spec = pl.BlockSpec((ROWBLK, feats), lambda row, step, table: (row, 0))
    flops = 6 * row_blocks * ROWBLK * feats * capacity * BLK
    return pl.pallas_call(
        functools.partial(parts_kernel, first, group),
        out_shape=jax.ShapeDtypeStruct((3, row_blocks * capacity * ROWBLK, BLK), jnp.float32),
        grid_spec=pltpu.PrefetchScalarGridSpec(
            num_scalar_prefetch=1,
            grid=(row_blocks, steps),
            in_specs=[rows_spec, rows_spec] + weight_specs(first, group, feats),
            out_specs=pl.BlockSpec(
                (3, group * ROWBLK, BLK), lambda row, step, table: (0, row * steps + step, 0)
            ),
        ),
        compiler_params=pltpu.CompilerParams(vmem_limit_bytes=PLAIN_LIMIT),
        cost_estimate=pl.CostEstimate(
            flops=flops, bytes_accessed=flops // ROWBLK, transcendentals=0
        ),
    )(table, tok, cot, *([gate_w] * group + [up_w] * group + [down_w] * group))


def exchange_kernel(
    count, inputs, *refs
):
    part_refs, all_ref = refs[:inputs], refs[inputs]
    (
        mine, paired, xsend, xland, zsend, zland, acts,
        load_sem, pair_send, pair_recv, x_send, x_recv, z_send, z_recv,
    up_send, down_send, side_send, all_recv, hand_send, hand_recv, own_sem,
    ) = refs[inputs + 1 :]
    _, _, subs, wide, tall, _, _ = part_refs[0].shape
    halves = inputs * subs
    chips = count // 2
    me = lax.axis_index("seq")
    chip, core = me // 2, lax.rem(me, 2)
    sibling = {"seq": me + 1 - 2 * core}
    along, across = chip // wide, lax.rem(chip, wide)
    order = sorted(range(1, tall), key=lambda shift: abs(2 * shift - tall))

    def device(i, j):
        return {"seq": (i * wide + j) * 2 + core}

    def column(shift):
        return lax.rem(across + shift, wide)

    def line(shift):
        return lax.rem(along + shift, tall)

    def remote(src, dst, send, recv, target):
        return pltpu.make_async_remote_copy(
            src_ref=src, dst_ref=dst, send_sem=send, recv_sem=recv,
            device_id=target, device_id_type=MESH,
        )

    barrier = pltpu.get_barrier_semaphore()
    pl.semaphore_signal(barrier, inc=1, device_id=sibling, device_id_type=MESH)
    for s in range(1, wide):
        pl.semaphore_signal(
            barrier, inc=1, device_id=device(along, column(s)), device_id_type=MESH
        )
    for d in range(1, tall):
        pl.semaphore_signal(barrier, inc=1, device_id=device(line(d), across), device_id_type=MESH)
    pl.semaphore_wait(barrier, wide + tall - 1)

    def part_at(h, s, d, side):
        return part_refs[h // subs].at[:, side, h % subs, column(s), line(d)]

    def load_copy(h, s, d):
        return pltpu.make_async_copy(
            part_at(h, s, d, core), mine.at[h, s, d], load_sem.at[h, s, d]
        )

    def pair_copy(h, s, d):
        return remote(
            part_at(h, s, d, 1 - core), paired.at[h, s, d],
            pair_send.at[h, s, d], pair_recv.at[h, s, d], sibling,
        )

    def x_copy(h, s, d):
        return remote(
            xsend.at[h, s - 1, d], xland.at[h, s - 1, d],
            x_send.at[h, s, d], x_recv.at[h, s, d], device(along, column(s)),
        )

    def z_copy(h, d):
        return remote(
            zsend.at[h, d - 1], zland.at[h, d - 1],
            z_send.at[h, d], z_recv.at[h, d], device(line(d), across),
        )

    def slot(h, i, j, side):
        return all_ref.at[h // subs, :, side, h % subs, j, i]

    def z_route(h, i, j, to, send, src=None):
        dst = slot(h, i, j, core)
        owner = i * wide + j
        return remote(
            dst if src is None else src, dst, send.at[h, owner], all_recv.at[h, owner],
            device(to, across),
        )

    def x_route(h, i, s, src=None):
        dst = slot(h, i, across, core)
        return remote(
            dst if src is None else src, dst, side_send.at[h, s, i],
            all_recv.at[h, i * wide + across], device(along, column(s)),
        )

    def hand_copy(h, i, j, side, src=None):
        dst = slot(h, i, j, side)
        owner = i * wide + j
        return remote(
            dst if src is None else src, dst, hand_send.at[h, owner], hand_recv.at[h, owner], sibling
        )

    def take(h, i, j):
        z_route(h, i, j, along, up_send).wait_recv()

    def pass_on(h, i, j, up, down, src=None):
        if up:

            @pl.when(along < tall - 1)
            def _():
                z_route(h, i, j, along + 1, up_send, src).start()

        if down:

            @pl.when(along > 0)
            def _():
                z_route(h, i, j, along - 1, down_send, src).start()

    def spread(h, i, src=None):
        for s in range(1, wide):
            x_route(h, i, s, src).start()

    for h in range(halves):
        for s in list(range(1, wide)) + [0]:
            for d in order + [0]:
                pair_copy(h, s, d).start()
                load_copy(h, s, d).start()

    for h in range(halves):
        for d in order + [0]:
            for s in range(1, wide):
                load_copy(h, s, d).wait()
                pair_copy(h, s, d).wait_recv()
                xsend[h, s - 1, d] = (mine[h, s, d] + paired[h, s, d]).astype(jnp.bfloat16)
                x_copy(h, s, d).start()

    def row_sum(h, d):
        load_copy(h, 0, d).wait()
        pair_copy(h, 0, d).wait_recv()
        total = mine[h, 0, d] + paired[h, 0, d]
        for s in range(1, wide):
            x_copy(h, s, d).wait_recv()
            total = total + xland[h, s - 1, d].astype(jnp.float32)
        return total

    for h in range(halves):
        for d in order:
            zsend[h, d - 1] = row_sum(h, d).astype(jnp.bfloat16)
            z_copy(h, d).start()

    def own_copy(h):
        return pltpu.make_async_copy(acts.at[h], slot(h, along, across, core), own_sem.at[h])

    for h in range(halves):
        total = row_sum(h, 0)
        for d in order:
            z_copy(h, d).wait_recv()
            total = total + zland[h, d - 1].astype(jnp.float32)
        gate, up, grad = total[0], total[1], total[2]
        sig = jax.nn.sigmoid(gate)
        acts[h, 0] = (gate * sig * up).astype(jnp.bfloat16)
        acts[h, 1] = (grad * up * sig * (1.0 + gate * (1.0 - sig))).astype(jnp.bfloat16)
        acts[h, 2] = (grad * gate * sig).astype(jnp.bfloat16)
        src = acts.at[h]
        pass_on(h, along, across, True, True, src)
        spread(h, along, src)
        hand_copy(h, along, across, core, src).start()
        own_copy(h).start()

    for h in range(halves):
        if h % 2 == 1:
            for s in range(1, wide):
                take(h, along, column(s))
                pass_on(h, along, column(s), True, True)
                hand_copy(h, along, column(s), core).start()
    for far in range(1, tall):
        for h in range(halves):
            for s in range(wide if h % 2 == 1 else 1):
                for sign in (-1, 1):

                    @pl.when(along >= far if sign < 0 else along + far < tall)
                    def _(h=h, s=s, sign=sign):
                        i = along + sign * far
                        take(h, i, column(s))
                        pass_on(h, i, column(s), sign < 0, sign > 0)
                        if h % 2 == 0:
                            spread(h, i)
                        hand_copy(h, i, column(s), core).start()

    for h in range(0, halves, 2):
        for s in range(1, wide):
            for d in [0] + list(range(1, tall)):
                take(h, line(d), column(s))
                hand_copy(h, line(d), column(s), core).start()

    for h in range(halves):
        own_copy(h).wait()

        def finish(owner, carry, h=h):
            i, j = owner // wide, lax.rem(owner, wide)
            hand_copy(h, i, j, 1 - core).wait_recv()
            hand_copy(h, i, j, core).wait_send()
            mine = jnp.bool_(True) if h % 2 == 1 else j == across

            @pl.when(jnp.logical_and(mine, jnp.logical_and(i <= along, along < tall - 1)))
            def _():
                z_route(h, i, j, along + 1, up_send).wait_send()

            @pl.when(jnp.logical_and(mine, jnp.logical_and(i >= along, along > 0)))
            def _():
                z_route(h, i, j, along - 1, down_send).wait_send()

            return carry

        lax.fori_loop(0, chips, finish, 0)
        for s in range(1, wide):
            if h % 2 == 1:
                x_route(h, along, s).wait_send()
            else:
                for i in range(tall):
                    x_route(h, i, s).wait_send()
        for d in range(tall):
            for s in range(wide):
                pair_copy(h, s, d).wait_send()
                if s > 0:
                    x_copy(h, s, d).wait_send()
            if d > 0:
                z_copy(h, d).wait_send()


def exchange(parts, collective_id):
    count = lax.axis_size("seq")
    chips = count // 2
    tall = 4 if chips % 4 == 0 else chips
    wide = chips // tall
    inputs = len(parts)
    own = parts[0].shape[1] // count
    subs = 2 if inputs == 1 and own % 32 == 0 else 1
    halves = inputs * subs
    piece = own // subs
    shape = (3, 2, subs, wide, tall, piece, BLK)
    chunk = (3, piece, BLK)
    dma = pltpu.SemaphoreType.DMA
    anywhere = pl.BlockSpec(memory_space=pl.ANY)
    out = pl.pallas_call(
        functools.partial(exchange_kernel, count, inputs),
        out_shape=jax.ShapeDtypeStruct((inputs,) + shape, jnp.bfloat16),
        in_specs=[anywhere] * inputs,
        out_specs=anywhere,
        scratch_shapes=[
            pltpu.VMEM((halves, wide, tall) + chunk, jnp.float32),
            pltpu.VMEM((halves, wide, tall) + chunk, jnp.float32),
            pltpu.VMEM((halves, max(wide - 1, 1), tall) + chunk, jnp.bfloat16),
            pltpu.VMEM((halves, max(wide - 1, 1), tall) + chunk, jnp.bfloat16),
            pltpu.VMEM((halves, max(tall - 1, 1)) + chunk, jnp.bfloat16),
            pltpu.VMEM((halves, max(tall - 1, 1)) + chunk, jnp.bfloat16),
            pltpu.VMEM((halves,) + chunk, jnp.bfloat16),
            dma((halves, wide, tall)),
            dma((halves, wide, tall)),
            dma((halves, wide, tall)),
            dma((halves, wide, tall)),
            dma((halves, wide, tall)),
            dma((halves, tall)),
            dma((halves, tall)),
            dma((halves, chips)),
            dma((halves, chips)),
            dma((halves, wide, tall)),
            dma((halves, chips)),
            dma((halves, chips)),
            dma((halves, chips)),
            dma((halves,)),
        ],
        compiler_params=pltpu.CompilerParams(
            collective_id=collective_id, has_side_effects=True, vmem_limit_bytes=COMM_LIMIT
        ),
    )(*(part.reshape(shape) for part in parts))
    return out.reshape((inputs,) + parts[0].shape)


def rows_out_kernel(group, table_ref, act_ref, *refs):
    gates, ups, downs = refs[:group], refs[group : 2 * group], refs[2 * group : 3 * group]
    out_ref = refs[3 * group]
    step = pl.program_id(1)

    @pl.when(step == 0)
    def _():
        out_ref[...] = jnp.zeros_like(out_ref)

    out = jnp.zeros(out_ref.shape[2:], jnp.float32)
    grad = jnp.zeros(out_ref.shape[2:], jnp.float32)
    across = (((1,), (1,)), ((), ()))
    for at in range(group):
        rows = slice(at * ROWBLK, (at + 1) * ROWBLK)
        out += jnp.dot(act_ref[0, 0, rows, :], downs[at][...], preferred_element_type=jnp.float32)
        grad += lax.dot_general(
            jnp.concatenate([act_ref[0, 1, rows, :], act_ref[0, 2, rows, :]], axis=1),
            jnp.concatenate([gates[at][...], ups[at][...]], axis=1),
            across,
            preferred_element_type=jnp.float32,
        )
    out_ref[0, 0] += out
    out_ref[0, 1] += grad


def rows_out(table, first, row_blocks, capacity, acts, gate_w, up_w, down_w):
    feats = gate_w.shape[0]
    group = group_of(capacity)
    steps = capacity // group
    if acts.shape[0] == row_blocks:
        place = lambda row, step, table: (row, 0, step, 0)
    else:
        place = lambda row, step, table: (0, 0, row * steps + step, 0)
    flops = 6 * row_blocks * ROWBLK * feats * capacity * BLK
    return pl.pallas_call(
        functools.partial(rows_out_kernel, group),
        out_shape=jax.ShapeDtypeStruct((row_blocks, 2, ROWBLK, feats), jnp.float32),
        grid_spec=pltpu.PrefetchScalarGridSpec(
            num_scalar_prefetch=1,
            grid=(row_blocks, steps),
            in_specs=[pl.BlockSpec((1, 3, group * ROWBLK, BLK), place)]
            + weight_specs(first, group, feats),
            out_specs=pl.BlockSpec((1, 2, ROWBLK, feats), lambda row, step, table: (row, 0, 0, 0)),
        ),
        compiler_params=pltpu.CompilerParams(vmem_limit_bytes=PLAIN_LIMIT),
        cost_estimate=pl.CostEstimate(
            flops=flops, bytes_accessed=flops // ROWBLK, transcendentals=0
        ),
    )(table, acts, *([gate_w] * group + [up_w] * group + [down_w] * group))


def weights_out_kernel(first, capacity, scale, pieces, table_ref, *refs):
    toks, cots = refs[:pieces], refs[pieces : 2 * pieces]
    act_ref, gate_ref, up_ref, down_ref, flipped, cot_all, dense = refs[2 * pieces :]
    step = pl.program_id(0)
    rows = flipped.shape[1]
    row_blocks = rows // ROWBLK
    group = gate_ref.shape[1] // BLK
    each = rows // pieces

    @pl.when(step == 0)
    def _():
        for at in range(pieces):
            cut = slice(at * each, (at + 1) * each)
            flipped[:, cut] = toks[at][...].T
            cot_all[cut, :] = cots[at][...]

    for at in range(group):
        for row in range(row_blocks):
            unit = table_ref[first + row, capacity + 1 + step * group + at]
            lead, base = (row, 0) if act_ref.shape[0] == row_blocks else (0, row * capacity)
            taken = pl.ds(pl.multiple_of((jnp.maximum(unit, 0) + base) * ROWBLK, ROWBLK), ROWBLK)
            for which in range(3):
                value = act_ref[lead, which, taken, :]
                dense[which, row * ROWBLK : (row + 1) * ROWBLK, at * BLK : (at + 1) * BLK] = (
                    jnp.where(unit >= 0, value, jnp.zeros_like(value))
                )
    tok = flipped[...]
    gate_ref[...] = jnp.dot(tok, dense[1], preferred_element_type=jnp.float32) * scale
    up_ref[...] = jnp.dot(tok, dense[2], preferred_element_type=jnp.float32) * scale
    down_ref[...] = (
        lax.dot_general(
            dense[0], cot_all[...], (((0,), (0,)), ((), ())), preferred_element_type=jnp.float32
        )
        * scale
    )


def weights_out(table, first, capacity, toks, cots, acts, scale):
    blocks = table.shape[1] - capacity - 1
    feats = toks[0].shape[1]
    pieces = len(toks)
    rows = pieces * toks[0].shape[0]
    group = group_of(blocks)
    whole = pl.BlockSpec(toks[0].shape, lambda step, table: (0, 0))
    wide = pl.BlockSpec((feats, group * BLK), lambda step, table: (0, step))
    hidden = blocks * BLK
    return pl.pallas_call(
        functools.partial(weights_out_kernel, first, capacity, scale, pieces),
        out_shape=(
            jax.ShapeDtypeStruct((feats, hidden), jnp.float32),
            jax.ShapeDtypeStruct((feats, hidden), jnp.float32),
            jax.ShapeDtypeStruct((hidden, feats), jnp.float32),
        ),
        grid_spec=pltpu.PrefetchScalarGridSpec(
            num_scalar_prefetch=1,
            grid=(blocks // group,),
            in_specs=[whole] * (2 * pieces)
            + [pl.BlockSpec(acts.shape, lambda step, table: (0, 0, 0, 0))],
            out_specs=(
                wide,
                wide,
                pl.BlockSpec((group * BLK, feats), lambda step, table: (step, 0)),
            ),
            scratch_shapes=[
                pltpu.VMEM((feats, rows), jnp.bfloat16),
                pltpu.VMEM((rows, feats), jnp.bfloat16),
                pltpu.VMEM((3, rows, group * BLK), jnp.bfloat16),
            ],
        ),
        compiler_params=pltpu.CompilerParams(vmem_limit_bytes=WIDE_LIMIT),
        cost_estimate=pl.CostEstimate(
            flops=6 * rows * feats * hidden, bytes_accessed=12 * feats * hidden, transcendentals=0
        ),
    )(table, *toks, *cots, acts)


def shards(tokens, gate_weight, up_weight, down_weight, masks, cotangent):
    tp_count = lax.axis_size("tp")
    rank = lax.axis_index("tp")
    rows, feats = tokens.shape
    total_rows = rows * tp_count
    row_blocks, blocks = masks.shape
    kept_total = blocks * tp_count // KEEP_PART
    capacity = min(2 * kept_total // tp_count, blocks)
    scale = 1.0 / math.sqrt(total_rows)
    weights = (gate_weight, up_weight, down_weight)

    if tp_count != 2 or row_blocks != 2 or rows != ROWBLK:
        table, _ = unit_tables(masks, jnp.int32(0), capacity)
        tok, cot = (value.reshape(total_rows, feats) for value in gather_rows(tokens, cotangent))
        parts = partial_products(table, 0, capacity, tok, cot, *weights)
        acts = exchange([parts], 1)
        row_parts = rows_out(table, 0, row_blocks, capacity, acts, *weights)
        row_parts = jnp.swapaxes(row_parts.reshape(tp_count, rows // ROWBLK, 2, ROWBLK, feats), 1, 2)
        moved = []
        for shift in range(1, tp_count):
            piece = lax.dynamic_index_in_dim(
                row_parts, lax.rem(rank + shift, tp_count), 0, keepdims=False
            ).astype(jnp.bfloat16)
            pairs = [(src, (src + shift) % tp_count) for src in range(tp_count)]
            moved.append(lax.ppermute(piece, "tp", pairs))
        grads = weights_out(table, 0, capacity, [tok], [cot], acts, scale)
        mine = lax.dynamic_index_in_dim(row_parts, rank, 0, keepdims=False)
        for piece in moved:
            mine = mine + piece.astype(jnp.float32)
        mine = mine.reshape(2, rows, feats).astype(jnp.bfloat16)
        return (mine[0], mine[1]) + tuple(grads)

    table, case = unit_tables(masks, rank, capacity)

    def swap(value):
        return lax.ppermute(value, "tp", [(0, 1), (1, 0)])

    def one_row(own, _):
        tok, cot = (tokens, cotangent) if own else (swap(tokens), swap(cotangent))
        first = 0 if own else 1
        parts = partial_products(table, first, capacity, tok, cot, *weights)
        acts = exchange([parts], 2 + first)
        sums = rows_out(table, first, 1, capacity, acts, *weights)[0].astype(jnp.bfloat16)
        if not own:
            sums = swap(sums)
        grads = weights_out(table, first, capacity, [tok], [cot], acts, scale)
        return (sums[0], sums[1]) + tuple(grads)

    def both_rows(_):
        tok, cot = swap(tokens), swap(cotangent)
        mine = partial_products(table, 0, capacity, tokens, cotangent, *weights)
        other = partial_products(table, 1, capacity, tok, cot, *weights)
        acts = exchange([mine, other], 1)
        sums = rows_out(table, 0, 2, capacity, acts, *weights)
        moved = swap(sums[1].astype(jnp.bfloat16))
        grads = weights_out(table, 0, capacity, [tokens, tok], [cotangent, cot], acts, scale)
        total = (sums[0] + moved.astype(jnp.float32)).astype(jnp.bfloat16)
        return (total[0], total[1]) + tuple(grads)

    return lax.switch(
        case[0],
        [functools.partial(one_row, True), functools.partial(one_row, False), both_rows],
        None,
    )


def solution(mesh):
    placed = (
        P("tp", "seq"),
        P("seq", "tp"),
        P("seq", "tp"),
        P("tp", "seq"),
        P(None, "tp"),
        P("tp", "seq"),
    )
    return jax.shard_map(
        shards,
        mesh=mesh,
        in_specs=placed,
        out_specs=(P("tp", "seq"), P("tp", "seq"), P("seq", "tp"), P("seq", "tp"), P("tp", "seq")),
        check_vma=False,
    )
```

```python
import functools
import math

import jax
import jax.numpy as jnp
from jax import lax
from jax.experimental import pallas as pl
from jax.experimental.pallas import tpu as pltpu
from jax.sharding import PartitionSpec as P

BLK = 128
ROWBLK = 128
KEEP_PART = 4
MESH = pl.DeviceIdType.MESH
PLAIN_LIMIT = 20 * 1024 * 1024
COMM_LIMIT = 28 * 1024 * 1024
WIDE_LIMIT = 32 * 1024 * 1024
FUSED_LIMIT = 60 * 1024 * 1024


def group_of(count):
    for size in (7, 8, 4, 2):
        if count % size == 0:
            return size
    return 1


def tables_kernel(capacity, first_ref, mask_ref, table_ref, index_ref, case_ref):
    row_blocks, blocks = mask_ref.shape
    counts = []
    for row in range(row_blocks):
        source = lax.rem(first_ref[0] + row, row_blocks)
        for slot in range(capacity + 1):
            table_ref[row, slot] = -1
            index_ref[row, slot] = 0

        def step(block, taken, row=row, source=source):
            kept = mask_ref[source, block]
            at = jnp.minimum(taken, capacity)
            table_ref[row, at] = jnp.where(kept == 1, block, -1)
            index_ref[row, at] = jnp.where(kept == 1, block, 0)
            table_ref[row, capacity + 1 + block] = jnp.where(kept == 1, at, -1)
            return taken + kept

        counts.append(lax.fori_loop(0, blocks, step, jnp.int32(0), unroll=8))
    mine, other = counts[0] > 0, counts[row_blocks - 1] > 0
    case_ref[0] = jnp.where(mine == other, 2, jnp.where(mine, 0, 1))


def unit_tables(masks, first, capacity):
    row_blocks, blocks = masks.shape
    smem = pl.BlockSpec(memory_space=pltpu.SMEM)
    return pl.pallas_call(
        functools.partial(tables_kernel, capacity),
        out_shape=(
            jax.ShapeDtypeStruct((row_blocks, capacity + 1 + blocks), jnp.int32),
            jax.ShapeDtypeStruct((row_blocks, capacity + 1), jnp.int32),
            jax.ShapeDtypeStruct((1,), jnp.int32),
        ),
        in_specs=[smem, smem],
        out_specs=(smem, smem, smem),
    )(first.reshape(1), masks)


def rows_kernel(count, tok_ref, cot_ref, tok_all, cot_all, send_sem, recv_sem, own_sem):
    me = lax.axis_index("tp")
    barrier = pltpu.get_barrier_semaphore()
    for shift in range(1, count):
        pl.semaphore_signal(
            barrier, inc=1, device_id={"tp": lax.rem(me + shift, count)}, device_id_type=MESH
        )
    pl.semaphore_wait(barrier, count - 1)
    copies = []
    for which, (src, dst) in enumerate(((tok_ref, tok_all), (cot_ref, cot_all))):
        for shift in range(1, count):
            copy = pltpu.make_async_remote_copy(
                src_ref=src,
                dst_ref=dst.at[me],
                send_sem=send_sem.at[which, shift],
                recv_sem=recv_sem.at[which, shift],
                device_id={"tp": lax.rem(me + shift, count)},
                device_id_type=MESH,
            )
            copy.start()
            copies.append(copy)
        own = pltpu.make_async_copy(src, dst.at[me], own_sem.at[which])
        own.start()
        copies.append(own)
    for copy in copies:
        copy.wait()


def gather_rows(tokens, cotangent):
    count = lax.axis_size("tp")
    rows, feats = tokens.shape
    anywhere = pl.BlockSpec(memory_space=pl.ANY)
    return pl.pallas_call(
        functools.partial(rows_kernel, count),
        out_shape=(jax.ShapeDtypeStruct((count, rows, feats), tokens.dtype),) * 2,
        in_specs=[anywhere] * 2,
        out_specs=(anywhere,) * 2,
        scratch_shapes=[
            pltpu.SemaphoreType.DMA((2, count)),
            pltpu.SemaphoreType.DMA((2, count)),
            pltpu.SemaphoreType.DMA((2,)),
        ],
        compiler_params=pltpu.CompilerParams(collective_id=0, has_side_effects=True),
    )(tokens, cotangent)


def parts_kernel(first, group, table_ref, tok_ref, cot_ref, *refs):
    gates, ups, downs = refs[:group], refs[group : 2 * group], refs[2 * group : 3 * group]
    out_ref = refs[3 * group]
    row, step = pl.program_id(0) + first, pl.program_id(1)
    tok, cot = tok_ref[...], cot_ref[...]
    for at in range(group):
        live = table_ref[row, step * group + at] >= 0
        rows = slice(at * ROWBLK, (at + 1) * ROWBLK)
        both = jnp.dot(
            tok,
            jnp.concatenate([gates[at][...], ups[at][...]], axis=1),
            preferred_element_type=jnp.float32,
        )
        grad = lax.dot_general(
            cot, downs[at][...], (((1,), (1,)), ((), ())), preferred_element_type=jnp.float32
        )
        out_ref[0, rows, :] = both[:, :BLK]
        out_ref[1, rows, :] = jnp.where(live, both[:, BLK:], 0.0)
        out_ref[2, rows, :] = jnp.where(live, grad, 0.0)


def weight_specs(first, group, feats):
    def block(table, row, step, at):
        return jnp.maximum(table[row + first, step * group + at], 0)

    def columns(at):
        return pl.BlockSpec((feats, BLK), lambda row, step, table: (0, block(table, row, step, at)))

    def rows(at):
        return pl.BlockSpec((BLK, feats), lambda row, step, table: (block(table, row, step, at), 0))

    return (
        [columns(at) for at in range(group)] * 2 + [rows(at) for at in range(group)]
    )


def partial_products(table, first, capacity, tok, cot, gate_w, up_w, down_w):
    row_blocks, feats = tok.shape[0] // ROWBLK, tok.shape[1]
    group = group_of(capacity)
    steps = capacity // group
    rows_spec = pl.BlockSpec((ROWBLK, feats), lambda row, step, table: (row, 0))
    flops = 6 * row_blocks * ROWBLK * feats * capacity * BLK
    return pl.pallas_call(
        functools.partial(parts_kernel, first, group),
        out_shape=jax.ShapeDtypeStruct((3, row_blocks * capacity * ROWBLK, BLK), jnp.float32),
        grid_spec=pltpu.PrefetchScalarGridSpec(
            num_scalar_prefetch=1,
            grid=(row_blocks, steps),
            in_specs=[rows_spec, rows_spec] + weight_specs(first, group, feats),
            out_specs=pl.BlockSpec(
                (3, group * ROWBLK, BLK), lambda row, step, table: (0, row * steps + step, 0)
            ),
        ),
        compiler_params=pltpu.CompilerParams(vmem_limit_bytes=PLAIN_LIMIT),
        cost_estimate=pl.CostEstimate(
            flops=flops, bytes_accessed=flops // ROWBLK, transcendentals=0
        ),
    )(table, tok, cot, *([gate_w] * group + [up_w] * group + [down_w] * group))


def exchange_kernel(
    count, inputs, *refs
):
    part_refs, all_ref = refs[:inputs], refs[inputs]
    (
        mine, paired, xsend, xland, zsend, zland, acts,
        load_sem, pair_send, pair_recv, x_send, x_recv, z_send, z_recv,
    up_send, down_send, side_send, all_recv, hand_send, hand_recv, own_sem,
    ) = refs[inputs + 1 :]
    _, _, subs, wide, tall, _, _ = part_refs[0].shape
    halves = inputs * subs
    chips = count // 2
    me = lax.axis_index("seq")
    chip, core = me // 2, lax.rem(me, 2)
    sibling = {"seq": me + 1 - 2 * core}
    along, across = chip // wide, lax.rem(chip, wide)
    order = sorted(range(1, tall), key=lambda shift: abs(2 * shift - tall))

    def device(i, j):
        return {"seq": (i * wide + j) * 2 + core}

    def column(shift):
        return lax.rem(across + shift, wide)

    def line(shift):
        return lax.rem(along + shift, tall)

    def remote(src, dst, send, recv, target):
        return pltpu.make_async_remote_copy(
            src_ref=src, dst_ref=dst, send_sem=send, recv_sem=recv,
            device_id=target, device_id_type=MESH,
        )

    barrier = pltpu.get_barrier_semaphore()
    pl.semaphore_signal(barrier, inc=1, device_id=sibling, device_id_type=MESH)
    for s in range(1, wide):
        pl.semaphore_signal(
            barrier, inc=1, device_id=device(along, column(s)), device_id_type=MESH
        )
    for d in range(1, tall):
        pl.semaphore_signal(barrier, inc=1, device_id=device(line(d), across), device_id_type=MESH)
    pl.semaphore_wait(barrier, wide + tall - 1)

    def part_at(h, s, d, side):
        return part_refs[h // subs].at[:, side, h % subs, column(s), line(d)]

    def load_copy(h, s, d):
        return pltpu.make_async_copy(
            part_at(h, s, d, core), mine.at[h, s, d], load_sem.at[h, s, d]
        )

    def pair_copy(h, s, d):
        return remote(
            part_at(h, s, d, 1 - core), paired.at[h, s, d],
            pair_send.at[h, s, d], pair_recv.at[h, s, d], sibling,
        )

    def x_copy(h, s, d):
        return remote(
            xsend.at[h, s - 1, d], xland.at[h, s - 1, d],
            x_send.at[h, s, d], x_recv.at[h, s, d], device(along, column(s)),
        )

    def z_copy(h, d):
        return remote(
            zsend.at[h, d - 1], zland.at[h, d - 1],
            z_send.at[h, d], z_recv.at[h, d], device(line(d), across),
        )

    def slot(h, i, j, side):
        return all_ref.at[h // subs, :, side, h % subs, j, i]

    def z_route(h, i, j, to, send, src=None):
        dst = slot(h, i, j, core)
        owner = i * wide + j
        return remote(
            dst if src is None else src, dst, send.at[h, owner], all_recv.at[h, owner],
            device(to, across),
        )

    def x_route(h, i, s, src=None):
        dst = slot(h, i, across, core)
        return remote(
            dst if src is None else src, dst, side_send.at[h, s, i],
            all_recv.at[h, i * wide + across], device(along, column(s)),
        )

    def hand_copy(h, i, j, side, src=None):
        dst = slot(h, i, j, side)
        owner = i * wide + j
        return remote(
            dst if src is None else src, dst, hand_send.at[h, owner], hand_recv.at[h, owner], sibling
        )

    def take(h, i, j):
        z_route(h, i, j, along, up_send).wait_recv()

    def pass_on(h, i, j, up, down, src=None):
        if up:

            @pl.when(along < tall - 1)
            def _():
                z_route(h, i, j, along + 1, up_send, src).start()

        if down:

            @pl.when(along > 0)
            def _():
                z_route(h, i, j, along - 1, down_send, src).start()

    def spread(h, i, src=None):
        for s in range(1, wide):
            x_route(h, i, s, src).start()

    for h in range(halves):
        for s in list(range(1, wide)) + [0]:
            for d in order + [0]:
                pair_copy(h, s, d).start()
                load_copy(h, s, d).start()

    for h in range(halves):
        for d in order + [0]:
            for s in range(1, wide):
                load_copy(h, s, d).wait()
                pair_copy(h, s, d).wait_recv()
                xsend[h, s - 1, d] = (mine[h, s, d] + paired[h, s, d]).astype(jnp.bfloat16)
                x_copy(h, s, d).start()

    def row_sum(h, d):
        load_copy(h, 0, d).wait()
        pair_copy(h, 0, d).wait_recv()
        total = mine[h, 0, d] + paired[h, 0, d]
        for s in range(1, wide):
            x_copy(h, s, d).wait_recv()
            total = total + xland[h, s - 1, d].astype(jnp.float32)
        return total

    for h in range(halves):
        for d in order:
            zsend[h, d - 1] = row_sum(h, d).astype(jnp.bfloat16)
            z_copy(h, d).start()

    def own_copy(h):
        return pltpu.make_async_copy(acts.at[h], slot(h, along, across, core), own_sem.at[h])

    for h in range(halves):
        total = row_sum(h, 0)
        for d in order:
            z_copy(h, d).wait_recv()
            total = total + zland[h, d - 1].astype(jnp.float32)
        gate, up, grad = total[0], total[1], total[2]
        sig = jax.nn.sigmoid(gate)
        acts[h, 0] = (gate * sig * up).astype(jnp.bfloat16)
        acts[h, 1] = (grad * up * sig * (1.0 + gate * (1.0 - sig))).astype(jnp.bfloat16)
        acts[h, 2] = (grad * gate * sig).astype(jnp.bfloat16)
        src = acts.at[h]
        pass_on(h, along, across, True, True, src)
        spread(h, along, src)
        hand_copy(h, along, across, core, src).start()
        own_copy(h).start()

    for h in range(halves):
        if h % 2 == 1:
            for s in range(1, wide):
                take(h, along, column(s))
                pass_on(h, along, column(s), True, True)
                hand_copy(h, along, column(s), core).start()
    for far in range(1, tall):
        for h in range(halves):
            for s in range(wide if h % 2 == 1 else 1):
                for sign in (-1, 1):

                    @pl.when(along >= far if sign < 0 else along + far < tall)
                    def _(h=h, s=s, sign=sign):
                        i = along + sign * far
                        take(h, i, column(s))
                        pass_on(h, i, column(s), sign < 0, sign > 0)
                        if h % 2 == 0:
                            spread(h, i)
                        hand_copy(h, i, column(s), core).start()

    for h in range(0, halves, 2):
        for s in range(1, wide):
            for d in [0] + list(range(1, tall)):
                take(h, line(d), column(s))
                hand_copy(h, line(d), column(s), core).start()

    for h in range(halves):
        own_copy(h).wait()

        def finish(owner, carry, h=h):
            i, j = owner // wide, lax.rem(owner, wide)
            hand_copy(h, i, j, 1 - core).wait_recv()
            hand_copy(h, i, j, core).wait_send()
            mine = jnp.bool_(True) if h % 2 == 1 else j == across

            @pl.when(jnp.logical_and(mine, jnp.logical_and(i <= along, along < tall - 1)))
            def _():
                z_route(h, i, j, along + 1, up_send).wait_send()

            @pl.when(jnp.logical_and(mine, jnp.logical_and(i >= along, along > 0)))
            def _():
                z_route(h, i, j, along - 1, down_send).wait_send()

            return carry

        lax.fori_loop(0, chips, finish, 0)
        for s in range(1, wide):
            if h % 2 == 1:
                x_route(h, along, s).wait_send()
            else:
                for i in range(tall):
                    x_route(h, i, s).wait_send()
        for d in range(tall):
            for s in range(wide):
                pair_copy(h, s, d).wait_send()
                if s > 0:
                    x_copy(h, s, d).wait_send()
            if d > 0:
                z_copy(h, d).wait_send()


def exchange(parts, collective_id):
    count = lax.axis_size("seq")
    chips = count // 2
    tall = 4 if chips % 4 == 0 else chips
    wide = chips // tall
    inputs = len(parts)
    own = parts[0].shape[1] // count
    subs = 2 if inputs == 1 and own % 32 == 0 else 1
    halves = inputs * subs
    piece = own // subs
    shape = (3, 2, subs, wide, tall, piece, BLK)
    chunk = (3, piece, BLK)
    dma = pltpu.SemaphoreType.DMA
    anywhere = pl.BlockSpec(memory_space=pl.ANY)
    out = pl.pallas_call(
        functools.partial(exchange_kernel, count, inputs),
        out_shape=jax.ShapeDtypeStruct((inputs,) + shape, jnp.bfloat16),
        in_specs=[anywhere] * inputs,
        out_specs=anywhere,
        scratch_shapes=[
            pltpu.VMEM((halves, wide, tall) + chunk, jnp.float32),
            pltpu.VMEM((halves, wide, tall) + chunk, jnp.float32),
            pltpu.VMEM((halves, max(wide - 1, 1), tall) + chunk, jnp.bfloat16),
            pltpu.VMEM((halves, max(wide - 1, 1), tall) + chunk, jnp.bfloat16),
            pltpu.VMEM((halves, max(tall - 1, 1)) + chunk, jnp.bfloat16),
            pltpu.VMEM((halves, max(tall - 1, 1)) + chunk, jnp.bfloat16),
            pltpu.VMEM((halves,) + chunk, jnp.bfloat16),
            dma((halves, wide, tall)),
            dma((halves, wide, tall)),
            dma((halves, wide, tall)),
            dma((halves, wide, tall)),
            dma((halves, wide, tall)),
            dma((halves, tall)),
            dma((halves, tall)),
            dma((halves, chips)),
            dma((halves, chips)),
            dma((halves, wide, tall)),
            dma((halves, chips)),
            dma((halves, chips)),
            dma((halves, chips)),
            dma((halves,)),
        ],
        compiler_params=pltpu.CompilerParams(
            collective_id=collective_id, has_side_effects=True, vmem_limit_bytes=COMM_LIMIT
        ),
    )(*(part.reshape(shape) for part in parts))
    return out.reshape((inputs,) + parts[0].shape)


def rows_out_kernel(group, table_ref, act_ref, *refs):
    gates, ups, downs = refs[:group], refs[group : 2 * group], refs[2 * group : 3 * group]
    out_ref = refs[3 * group]
    step = pl.program_id(1)

    @pl.when(step == 0)
    def _():
        out_ref[...] = jnp.zeros_like(out_ref)

    out = jnp.zeros(out_ref.shape[2:], jnp.float32)
    grad = jnp.zeros(out_ref.shape[2:], jnp.float32)
    across = (((1,), (1,)), ((), ()))
    for at in range(group):
        rows = slice(at * ROWBLK, (at + 1) * ROWBLK)
        out += jnp.dot(act_ref[0, 0, rows, :], downs[at][...], preferred_element_type=jnp.float32)
        grad += lax.dot_general(
            jnp.concatenate([act_ref[0, 1, rows, :], act_ref[0, 2, rows, :]], axis=1),
            jnp.concatenate([gates[at][...], ups[at][...]], axis=1),
            across,
            preferred_element_type=jnp.float32,
        )
    out_ref[0, 0] += out
    out_ref[0, 1] += grad


def rows_out(table, first, row_blocks, capacity, acts, gate_w, up_w, down_w):
    feats = gate_w.shape[0]
    group = group_of(capacity)
    steps = capacity // group
    if acts.shape[0] == row_blocks:
        place = lambda row, step, table: (row, 0, step, 0)
    else:
        place = lambda row, step, table: (0, 0, row * steps + step, 0)
    flops = 6 * row_blocks * ROWBLK * feats * capacity * BLK
    return pl.pallas_call(
        functools.partial(rows_out_kernel, group),
        out_shape=jax.ShapeDtypeStruct((row_blocks, 2, ROWBLK, feats), jnp.float32),
        grid_spec=pltpu.PrefetchScalarGridSpec(
            num_scalar_prefetch=1,
            grid=(row_blocks, steps),
            in_specs=[pl.BlockSpec((1, 3, group * ROWBLK, BLK), place)]
            + weight_specs(first, group, feats),
            out_specs=pl.BlockSpec((1, 2, ROWBLK, feats), lambda row, step, table: (row, 0, 0, 0)),
        ),
        compiler_params=pltpu.CompilerParams(vmem_limit_bytes=PLAIN_LIMIT),
        cost_estimate=pl.CostEstimate(
            flops=flops, bytes_accessed=flops // ROWBLK, transcendentals=0
        ),
    )(table, acts, *([gate_w] * group + [up_w] * group + [down_w] * group))


def weights_out_kernel(first, capacity, scale, pieces, table_ref, *refs):
    toks, cots = refs[:pieces], refs[pieces : 2 * pieces]
    act_ref, gate_ref, up_ref, down_ref, flipped, cot_all, dense = refs[2 * pieces :]
    step = pl.program_id(0)
    rows = flipped.shape[1]
    row_blocks = rows // ROWBLK
    group = gate_ref.shape[1] // BLK
    each = rows // pieces
    held = act_ref.shape[2] // ROWBLK

    @pl.when(step == 0)
    def _():
        for at in range(pieces):
            cut = slice(at * each, (at + 1) * each)
            flipped[:, cut] = toks[at][...].T
            cot_all[cut, :] = cots[at][...]

    for at in range(group):
        for row in range(row_blocks):
            unit = table_ref[first + row, capacity + 1 + step * group + at]
            index = jnp.maximum(unit, 0) + row * capacity
            lead, index = index // held, lax.rem(index, held)
            taken = pl.ds(pl.multiple_of(index * ROWBLK, ROWBLK), ROWBLK)
            for which in range(3):
                value = act_ref[lead, which, taken, :]
                dense[which, row * ROWBLK : (row + 1) * ROWBLK, at * BLK : (at + 1) * BLK] = (
                    jnp.where(unit >= 0, value, jnp.zeros_like(value))
                )
    tok = flipped[...]
    gate_ref[...] = jnp.dot(tok, dense[1], preferred_element_type=jnp.float32) * scale
    up_ref[...] = jnp.dot(tok, dense[2], preferred_element_type=jnp.float32) * scale
    down_ref[...] = (
        lax.dot_general(
            dense[0], cot_all[...], (((0,), (0,)), ((), ())), preferred_element_type=jnp.float32
        )
        * scale
    )


def weights_out(table, first, capacity, toks, cots, acts, scale):
    blocks = table.shape[1] - capacity - 1
    feats = toks[0].shape[1]
    pieces = len(toks)
    rows = pieces * toks[0].shape[0]
    group = group_of(blocks)
    whole = pl.BlockSpec(toks[0].shape, lambda step, table: (0, 0))
    wide = pl.BlockSpec((feats, group * BLK), lambda step, table: (0, step))
    hidden = blocks * BLK
    return pl.pallas_call(
        functools.partial(weights_out_kernel, first, capacity, scale, pieces),
        out_shape=(
            jax.ShapeDtypeStruct((feats, hidden), jnp.float32),
            jax.ShapeDtypeStruct((feats, hidden), jnp.float32),
            jax.ShapeDtypeStruct((hidden, feats), jnp.float32),
        ),
        grid_spec=pltpu.PrefetchScalarGridSpec(
            num_scalar_prefetch=1,
            grid=(blocks // group,),
            in_specs=[whole] * (2 * pieces)
            + [pl.BlockSpec(acts.shape, lambda step, table: (0, 0, 0, 0))],
            out_specs=(
                wide,
                wide,
                pl.BlockSpec((group * BLK, feats), lambda step, table: (step, 0)),
            ),
            scratch_shapes=[
                pltpu.VMEM((feats, rows), jnp.bfloat16),
                pltpu.VMEM((rows, feats), jnp.bfloat16),
                pltpu.VMEM((3, rows, group * BLK), jnp.bfloat16),
            ],
        ),
        compiler_params=pltpu.CompilerParams(vmem_limit_bytes=WIDE_LIMIT),
        cost_estimate=pl.CostEstimate(
            flops=6 * rows * feats * hidden, bytes_accessed=12 * feats * hidden, transcendentals=0
        ),
    )(table, *toks, *cots, acts)


def fused_kernel(mode, count, *refs):
    swapped, both = mode == "other", mode == "both"
    moving = swapped or both
    table_ref, tok_ref, cot_ref, gate_hbm, up_hbm, down_hbm = refs[:6]
    acts_out, sums, tok_out, cot_out = (refs[6:10] if moving else refs[6:8] + (None, None))
    (
        gate_w, up_w, down_w, toks, cots, parts, paired, xsend, xland, zsend, zland, acts,
        weight_sem, row_send, row_recv, row_load, row_store, pair_send, pair_recv, x_send, x_recv,
        z_send, z_recv, up_send, down_send, side_send, all_recv, hand_send, hand_recv, out_sem,
    ) = refs[10 if moving else 8 :]
    groups, _, held, _ = parts.shape
    rows = toks.shape[0]
    first = 1 if swapped else 0
    units = held // ROWBLK
    _, wide, tall, _, piece, _ = paired.shape
    chips = count // 2
    me, rank = lax.axis_index("seq"), lax.axis_index("tp")
    chip, core = me // 2, lax.rem(me, 2)
    sibling, partner = {"seq": me + 1 - 2 * core}, {"tp": 1 - rank}
    along, across = chip // wide, lax.rem(chip, wide)
    order = sorted(range(1, tall), key=lambda shift: abs(2 * shift - tall))
    contract = (((1,), (1,)), ((), ()))

    def device(i, j):
        return {"seq": (i * wide + j) * 2 + core}

    def column(shift):
        return lax.rem(across + shift, wide)

    def line(shift):
        return lax.rem(along + shift, tall)

    def rows_of(side, i, j):
        return pl.ds(pl.multiple_of(((side * wide + j) * tall + i) * piece, 16), piece)

    def remote(src, dst, send, recv, target):
        return pltpu.make_async_remote_copy(
            src_ref=src, dst_ref=dst, send_sem=send, recv_sem=recv,
            device_id=target, device_id_type=MESH,
        )

    def signal(target):
        pl.semaphore_signal(
            pltpu.get_barrier_semaphore(), inc=1, device_id=target, device_id_type=MESH
        )

    blocks = down_w.shape[0]

    def start_block(block, carry):
        cut = pl.ds(pl.multiple_of(block * BLK, BLK), BLK)
        for at, (src, dst) in enumerate(
            (
                (gate_hbm.at[:, cut], gate_w),
                (up_hbm.at[:, cut], up_w),
                (down_hbm.at[cut, :], down_w),
            )
        ):
            pltpu.make_async_copy(src, dst.at[block], weight_sem.at[at]).start()
        return carry

    own_rows = [
        pltpu.make_async_copy(src, dst.at[0], row_load.at[at])
        for at, (src, dst) in enumerate(((tok_ref, toks), (cot_ref, cots)))
        if not swapped
    ]
    for copy in own_rows:
        copy.start()
    lax.fori_loop(0, blocks, start_block, 0)

    signal(sibling)
    for s in range(1, wide):
        signal(device(along, column(s)))
    for d in range(1, tall):
        signal(device(line(d), across))
    if moving:
        signal(partner)
    pl.semaphore_wait(pltpu.get_barrier_semaphore(), wide + tall - 1 + (1 if moving else 0))

    row_copies = [
        remote(src, dst.at[rows - 1], row_send.at[at], row_recv.at[at], partner)
        for at, (src, dst) in enumerate(((tok_ref, toks), (cot_ref, cots)))
        if moving
    ]
    for copy in row_copies:
        copy.start()
    row_stores = [
        pltpu.make_async_copy(src.at[rows - 1], dst, row_store.at[at])
        for at, (src, dst) in enumerate(((toks, tok_out), (cots, cot_out)))
        if moving
    ]

    def pair_copy(h, s, d):
        return remote(
            parts.at[h, :, rows_of(1 - core, line(d), column(s))], paired.at[h, s, d],
            pair_send.at[h, s, d], pair_recv.at[h, s, d], sibling,
        )

    def x_copy(h, s, d):
        return remote(
            xsend.at[h, s - 1, d], xland.at[h, s - 1, d],
            x_send.at[h, s, d], x_recv.at[h, s, d], device(along, column(s)),
        )

    def z_copy(h, d):
        return remote(
            zsend.at[h, d - 1], zland.at[h, d - 1],
            z_send.at[h, d], z_recv.at[h, d], device(line(d), across),
        )

    def slot(h, i, j, side):
        return acts.at[h, :, rows_of(side, i, j)]

    def z_route(h, i, j, to, send):
        dst, owner = slot(h, i, j, core), i * wide + j
        return remote(
            dst, dst, send.at[h, owner], all_recv.at[h, owner], device(to, across)
        )

    def x_route(h, i, s):
        dst = slot(h, i, across, core)
        return remote(
            dst, dst, side_send.at[h, s, i], all_recv.at[h, i * wide + across],
            device(along, column(s)),
        )

    def hand_copy(h, i, j, side):
        dst, owner = slot(h, i, j, side), i * wide + j
        return remote(dst, dst, hand_send.at[h, owner], hand_recv.at[h, owner], sibling)

    def out_copy(h):
        return pltpu.make_async_copy(acts.at[h], acts_out.at[h], out_sem.at[h])

    def take(h, i, j):
        z_route(h, i, j, along, up_send).wait_recv()

    def pass_on(h, i, j, up, down):
        if up:

            @pl.when(along < tall - 1)
            def _():
                z_route(h, i, j, along + 1, up_send).start()

        if down:

            @pl.when(along > 0)
            def _():
                z_route(h, i, j, along - 1, down_send).start()

    def spread(h, i):
        for s in range(1, wide):
            x_route(h, i, s).start()

    def line_first(h):
        return h != groups - 2

    def row_of(h):
        return h * rows // groups

    def block_of(h, unit):
        base = h % (groups // rows) * units
        return table_ref[first + row_of(h), base + unit]

    def unit_rows(unit):
        return pl.ds(pl.multiple_of(unit * ROWBLK, ROWBLK), ROWBLK)

    def multiply(h, low, high):
        def step(pair, carry):
            tok, cot = toks[row_of(h)], cots[row_of(h)]
            at = (unit_rows(2 * pair), unit_rows(2 * pair + 1))
            cut = (block_of(h, 2 * pair), block_of(h, 2 * pair + 1))
            for one in range(2):
                value = jnp.dot(
                    tok,
                    jnp.concatenate([gate_w[cut[one]], up_w[cut[one]]], axis=1),
                    preferred_element_type=jnp.float32,
                )
                parts[h, 0, at[one], :] = value[:, :BLK]
                parts[h, 1, at[one], :] = value[:, BLK:]
            grad = lax.dot_general(
                cot,
                jnp.concatenate([down_w[cut[0]], down_w[cut[1]]], axis=0),
                contract,
                preferred_element_type=jnp.float32,
            )
            parts[h, 2, at[0], :] = grad[:, :BLK]
            parts[h, 2, at[1], :] = grad[:, BLK:]
            return carry

        lax.fori_loop(low, high, step, 0)

    def pair_stage(h):
        for s in list(range(1, wide)) + [0]:
            for d in order + [0]:
                pair_copy(h, s, d).start()

    def x_stage(h):
        for d in order + [0]:
            for s in range(1, wide):
                pair_copy(h, s, d).wait_recv()
                xsend[h, s - 1, d] = (
                    parts[h, :, rows_of(core, line(d), column(s)), :] + paired[h, s, d]
                ).astype(jnp.bfloat16)
                x_copy(h, s, d).start()

    def row_sum(h, d):
        pair_copy(h, 0, d).wait_recv()
        total = parts[h, :, rows_of(core, line(d), across), :] + paired[h, 0, d]
        for s in range(1, wide):
            x_copy(h, s, d).wait_recv()
            total = total + xland[h, s - 1, d].astype(jnp.float32)
        return total

    def z_stage(h):
        for d in order:
            zsend[h, d - 1] = row_sum(h, d).astype(jnp.bfloat16)
            z_copy(h, d).start()

    def act_stage(h):
        total = row_sum(h, 0)
        for d in order:
            z_copy(h, d).wait_recv()
            total = total + zland[h, d - 1].astype(jnp.float32)
        gate, up, grad = total[0], total[1], total[2]
        sig = jax.nn.sigmoid(gate)
        own = rows_of(core, along, across)
        acts[h, 0, own, :] = (gate * sig * up).astype(jnp.bfloat16)
        acts[h, 1, own, :] = (grad * up * sig * (1.0 + gate * (1.0 - sig))).astype(jnp.bfloat16)
        acts[h, 2, own, :] = (grad * gate * sig).astype(jnp.bfloat16)
        pass_on(h, along, across, True, True)
        spread(h, along)
        hand_copy(h, along, across, core).start()

    def gather_stage(h, far):
        if far == 1 and not line_first(h):
            for s in range(1, wide):
                take(h, along, column(s))
                pass_on(h, along, column(s), True, True)
                hand_copy(h, along, column(s), core).start()
        for s in range(1 if line_first(h) else wide):
            for sign in (-1, 1):

                @pl.when(along >= far if sign < 0 else along + far < tall)
                def _(s=s, sign=sign):
                    i = along + sign * far
                    take(h, i, column(s))
                    pass_on(h, i, column(s), sign < 0, sign > 0)
                    if line_first(h):
                        spread(h, i)
                    hand_copy(h, i, column(s), core).start()

    def side_stage(h):
        if line_first(h):
            for s in range(1, wide):
                for d in range(tall):
                    take(h, line(d), column(s))
                    hand_copy(h, line(d), column(s), core).start()

    def sums_stage(h):
        def arrive(owner, carry):
            hand_copy(h, owner // wide, lax.rem(owner, wide), 1 - core).wait_recv()
            return carry

        lax.fori_loop(0, chips, arrive, 0)
        out_copy(h).start()
        row = row_of(h)

        def step(pair, carry):
            at = (unit_rows(2 * pair), unit_rows(2 * pair + 1))
            cut = (block_of(h, 2 * pair), block_of(h, 2 * pair + 1))
            sums[row, 0] += jnp.dot(
                jnp.concatenate([acts[h, 0, at[0], :], acts[h, 0, at[1], :]], axis=1),
                jnp.concatenate([down_w[cut[0]], down_w[cut[1]]], axis=0),
                preferred_element_type=jnp.float32,
            )
            grad = sums[row, 1]
            for one in range(2):
                grad += lax.dot_general(
                    jnp.concatenate([acts[h, 1, at[one], :], acts[h, 2, at[one], :]], axis=1),
                    jnp.concatenate([gate_w[cut[one]], up_w[cut[one]]], axis=1),
                    contract,
                    preferred_element_type=jnp.float32,
                )
            sums[row, 1] = grad
            return carry

        lax.fori_loop(0, units // 2, step, 0)

    sums[...] = jnp.zeros_like(sums)
    for copy in own_rows:
        copy.wait()
    for at, held_w in enumerate((gate_w, up_w, down_w)):
        pltpu.make_async_copy(held_w, held_w, weight_sem.at[at]).wait()
    half = (units // 2 + 1) // 2
    for h in range(groups):
        if moving and h == (0 if swapped else groups // 2):
            for copy in row_copies:
                copy.wait_recv()
            for copy in row_stores:
                copy.start()
        multiply(h, 0, half)
        if h > 0:
            x_stage(h - 1)
        multiply(h, half, units // 2)
        pair_stage(h)
    z_stage(0)
    x_stage(groups - 1)
    z_stage(1)
    last = tall + 1
    for turn in range(groups + last):
        for h in range(groups):
            at = turn - h
            if 1 <= at < tall:
                gather_stage(h, at)
            elif at == tall:
                side_stage(h)
            elif at == 0:
                act_stage(h)
        if turn + 2 < groups:
            z_stage(turn + 2)
        if 0 <= turn - last < groups:
            sums_stage(turn - last)

    for h in range(groups):

        def finish(owner, carry, h=h):
            i, j = owner // wide, lax.rem(owner, wide)
            hand_copy(h, i, j, core).wait_send()
            mine = j == across if line_first(h) else jnp.bool_(True)

            @pl.when(jnp.logical_and(mine, jnp.logical_and(i <= along, along < tall - 1)))
            def _():
                z_route(h, i, j, along + 1, up_send).wait_send()

            @pl.when(jnp.logical_and(mine, jnp.logical_and(i >= along, along > 0)))
            def _():
                z_route(h, i, j, along - 1, down_send).wait_send()

            return carry

        lax.fori_loop(0, chips, finish, 0)
        for s in range(1, wide):
            if line_first(h):
                for i in range(tall):
                    x_route(h, i, s).wait_send()
            else:
                x_route(h, along, s).wait_send()
        for d in range(tall):
            for s in range(wide):
                pair_copy(h, s, d).wait_send()
                if s > 0:
                    x_copy(h, s, d).wait_send()
            if d > 0:
                z_copy(h, d).wait_send()
        out_copy(h).wait()
    for copy in row_copies:
        copy.wait_send()
    for copy in row_stores:
        copy.wait()


def fused(mode, table, capacity, tok, cot, gate_w, up_w, down_w, collective_id):
    count = lax.axis_size("seq")
    chips = count // 2
    tall = 4 if chips % 4 == 0 else chips
    wide = chips // tall
    rows = 2 if mode == "both" else 1
    groups = 2 * rows
    feats, blocks = gate_w.shape[0], gate_w.shape[1] // BLK
    held = capacity // 2 * ROWBLK
    piece = held // count
    chunk = (3, piece, BLK)
    dma = pltpu.SemaphoreType.DMA
    anywhere = pl.BlockSpec(memory_space=pl.ANY)
    out_shape = [
        jax.ShapeDtypeStruct((groups, 3, held, BLK), jnp.bfloat16),
        jax.ShapeDtypeStruct((rows, 2) + tok.shape, jnp.float32),
    ]
    out_specs = [anywhere, pl.BlockSpec(memory_space=pltpu.VMEM)]
    if mode != "own":
        out_shape += [jax.ShapeDtypeStruct(tok.shape, tok.dtype)] * 2
        out_specs += [anywhere] * 2
    flops = 12 * rows * ROWBLK * tok.shape[1] * capacity * BLK
    return pl.pallas_call(
        functools.partial(fused_kernel, mode, count),
        out_shape=tuple(out_shape),
        in_specs=[pl.BlockSpec(memory_space=pltpu.SMEM)] + [anywhere] * 5,
        out_specs=tuple(out_specs),
        scratch_shapes=[
            pltpu.VMEM((blocks, feats, BLK), gate_w.dtype),
            pltpu.VMEM((blocks, feats, BLK), up_w.dtype),
            pltpu.VMEM((blocks, BLK, feats), down_w.dtype),
            pltpu.VMEM((rows,) + tok.shape, tok.dtype),
            pltpu.VMEM((rows,) + tok.shape, tok.dtype),
            pltpu.VMEM((groups, 3, held, BLK), jnp.float32),
            pltpu.VMEM((groups, wide, tall) + chunk, jnp.float32),
            pltpu.VMEM((groups, wide - 1, tall) + chunk, jnp.bfloat16),
            pltpu.VMEM((groups, wide - 1, tall) + chunk, jnp.bfloat16),
            pltpu.VMEM((groups, tall - 1) + chunk, jnp.bfloat16),
            pltpu.VMEM((groups, tall - 1) + chunk, jnp.bfloat16),
            pltpu.VMEM((groups, 3, held, BLK), jnp.bfloat16),
            dma((3,)),
            dma((2,)),
            dma((2,)),
            dma((2,)),
            dma((2,)),
            dma((groups, wide, tall)),
            dma((groups, wide, tall)),
            dma((groups, wide, tall)),
            dma((groups, wide, tall)),
            dma((groups, tall)),
            dma((groups, tall)),
            dma((groups, chips)),
            dma((groups, chips)),
            dma((groups, wide, tall)),
            dma((groups, chips)),
            dma((groups, chips)),
            dma((groups, chips)),
            dma((groups,)),
        ],
        compiler_params=pltpu.CompilerParams(
            collective_id=collective_id, has_side_effects=True, vmem_limit_bytes=FUSED_LIMIT
        ),
        cost_estimate=pl.CostEstimate(
            flops=flops, bytes_accessed=6 * gate_w.size, transcendentals=0
        ),
    )(table, tok, cot, gate_w, up_w, down_w)


def shards(tokens, gate_weight, up_weight, down_weight, masks, cotangent):
    tp_count = lax.axis_size("tp")
    seq_count = lax.axis_size("seq")
    rank = lax.axis_index("tp")
    rows, feats = tokens.shape
    total_rows = rows * tp_count
    row_blocks, blocks = masks.shape
    kept_total = blocks * tp_count // KEEP_PART
    capacity = min(2 * kept_total // tp_count, blocks)
    scale = 1.0 / math.sqrt(total_rows)
    weights = (gate_weight, up_weight, down_weight)

    fits = seq_count % 8 == 0 and capacity % 4 == 0 and capacity // 2 * ROWBLK % (16 * seq_count) == 0
    if tp_count != 2 or row_blocks != 2 or rows != ROWBLK or not fits:
        table, _, _ = unit_tables(masks, jnp.int32(0), capacity)
        tok, cot = (value.reshape(total_rows, feats) for value in gather_rows(tokens, cotangent))
        parts = partial_products(table, 0, capacity, tok, cot, *weights)
        acts = exchange([parts], 1)
        row_parts = rows_out(table, 0, row_blocks, capacity, acts, *weights)
        row_parts = jnp.swapaxes(row_parts.reshape(tp_count, rows // ROWBLK, 2, ROWBLK, feats), 1, 2)
        moved = []
        for shift in range(1, tp_count):
            piece = lax.dynamic_index_in_dim(
                row_parts, lax.rem(rank + shift, tp_count), 0, keepdims=False
            ).astype(jnp.bfloat16)
            pairs = [(src, (src + shift) % tp_count) for src in range(tp_count)]
            moved.append(lax.ppermute(piece, "tp", pairs))
        grads = weights_out(table, 0, capacity, [tok], [cot], acts, scale)
        mine = lax.dynamic_index_in_dim(row_parts, rank, 0, keepdims=False)
        for piece in moved:
            mine = mine + piece.astype(jnp.float32)
        mine = mine.reshape(2, rows, feats).astype(jnp.bfloat16)
        return (mine[0], mine[1]) + tuple(grads)

    table, index, case = unit_tables(masks, rank, capacity)

    def swap(value):
        return lax.ppermute(value, "tp", [(0, 1), (1, 0)])

    alive = table[0, 0] >= 0

    def one_row(own, _):
        first = 0 if own else 1
        acts, sums, *rest = fused(
            "own" if own else "other", index, capacity, tokens, cotangent, *weights, 2 + first
        )
        tok, cot = (tokens, cotangent) if own else rest
        sums = sums[0].astype(jnp.bfloat16)
        if not own:
            sums = swap(sums)
        grads = weights_out(table, first, capacity, [tok], [cot], acts, scale)
        return (sums[0], sums[1]) + tuple(grads)

    def both_rows(_):
        acts, sums, tok, cot = fused("both", index, capacity, tokens, cotangent, *weights, 1)
        sums = jnp.where(alive, sums, 0.0)
        moved = swap(sums[1].astype(jnp.bfloat16))
        grads = weights_out(table, 0, capacity, [tokens, tok], [cotangent, cot], acts, scale)
        total = (sums[0] + moved.astype(jnp.float32)).astype(jnp.bfloat16)
        return (total[0], total[1]) + tuple(grads)

    return lax.switch(
        case[0],
        [functools.partial(one_row, True), functools.partial(one_row, False), both_rows],
        None,
    )


def solution(mesh):
    placed = (
        P("tp", "seq"),
        P("seq", "tp"),
        P("seq", "tp"),
        P("tp", "seq"),
        P(None, "tp"),
        P("tp", "seq"),
    )
    return jax.shard_map(
        shards,
        mesh=mesh,
        in_specs=placed,
        out_specs=(P("tp", "seq"), P("tp", "seq"), P("seq", "tp"), P("seq", "tp"), P("tp", "seq")),
        check_vma=False,
    )
```

```python
import functools
import math

import jax
import jax.numpy as jnp
from jax import lax
from jax.experimental import pallas as pl
from jax.experimental.pallas import tpu as pltpu
from jax.sharding import PartitionSpec as P

BLK = 128
ROWBLK = 128
KEEP_PART = 4
MESH = pl.DeviceIdType.MESH
PLAIN_LIMIT = 20 * 1024 * 1024
COMM_LIMIT = 28 * 1024 * 1024
WIDE_LIMIT = 60 * 1024 * 1024
FUSED_LIMIT = 60 * 1024 * 1024


def group_of(count):
    for size in (7, 8, 4, 2):
        if count % size == 0:
            return size
    return 1


def wide_group(count):
    for size in (7, 8, 4, 2):
        if count % size == 0:
            return size
    return 1


def tables_kernel(capacity, first_ref, mask_ref, table_ref, index_ref, case_ref):
    row_blocks, blocks = mask_ref.shape
    sources = [lax.rem(first_ref[0] + row, row_blocks) for row in range(row_blocks)]

    def clear(slot, carry):
        for row in range(row_blocks):
            table_ref[row, slot] = -1
            index_ref[row, slot] = 0
        return carry

    lax.fori_loop(0, capacity + 1, clear, 0, unroll=True)

    def step(block, taken):
        following = []
        for row in range(row_blocks):
            kept = mask_ref[sources[row], block]
            at = jnp.minimum(taken[row], capacity)
            table_ref[row, at] = jnp.where(kept == 1, block, -1)
            index_ref[row, at] = jnp.where(kept == 1, block, 0)
            table_ref[row, capacity + 1 + block] = jnp.where(kept == 1, at, -1)
            following.append(taken[row] + kept)
        return tuple(following)

    counts = lax.fori_loop(0, blocks, step, (jnp.int32(0),) * row_blocks, unroll=8)
    for row in range(row_blocks):
        index_ref[row, capacity] = jnp.minimum(counts[row], 1)
    mine, other = counts[0] > 0, counts[row_blocks - 1] > 0
    case_ref[0] = jnp.where(mine == other, 2, jnp.where(mine, 0, 1))


def unit_tables(masks, first, capacity):
    row_blocks, blocks = masks.shape
    smem = pl.BlockSpec(memory_space=pltpu.SMEM)
    return pl.pallas_call(
        functools.partial(tables_kernel, capacity),
        out_shape=(
            jax.ShapeDtypeStruct((row_blocks, capacity + 1 + blocks), jnp.int32),
            jax.ShapeDtypeStruct((row_blocks, capacity + 1), jnp.int32),
            jax.ShapeDtypeStruct((1,), jnp.int32),
        ),
        in_specs=[smem, smem],
        out_specs=(smem, smem, smem),
    )(first.reshape(1), masks)


def rows_kernel(count, tok_ref, cot_ref, tok_all, cot_all, send_sem, recv_sem, own_sem):
    me = lax.axis_index("tp")
    barrier = pltpu.get_barrier_semaphore()
    for shift in range(1, count):
        pl.semaphore_signal(
            barrier, inc=1, device_id={"tp": lax.rem(me + shift, count)}, device_id_type=MESH
        )
    pl.semaphore_wait(barrier, count - 1)
    copies = []
    for which, (src, dst) in enumerate(((tok_ref, tok_all), (cot_ref, cot_all))):
        for shift in range(1, count):
            copy = pltpu.make_async_remote_copy(
                src_ref=src,
                dst_ref=dst.at[me],
                send_sem=send_sem.at[which, shift],
                recv_sem=recv_sem.at[which, shift],
                device_id={"tp": lax.rem(me + shift, count)},
                device_id_type=MESH,
            )
            copy.start()
            copies.append(copy)
        own = pltpu.make_async_copy(src, dst.at[me], own_sem.at[which])
        own.start()
        copies.append(own)
    for copy in copies:
        copy.wait()


def gather_rows(tokens, cotangent):
    count = lax.axis_size("tp")
    rows, feats = tokens.shape
    anywhere = pl.BlockSpec(memory_space=pl.ANY)
    return pl.pallas_call(
        functools.partial(rows_kernel, count),
        out_shape=(jax.ShapeDtypeStruct((count, rows, feats), tokens.dtype),) * 2,
        in_specs=[anywhere] * 2,
        out_specs=(anywhere,) * 2,
        scratch_shapes=[
            pltpu.SemaphoreType.DMA((2, count)),
            pltpu.SemaphoreType.DMA((2, count)),
            pltpu.SemaphoreType.DMA((2,)),
        ],
        compiler_params=pltpu.CompilerParams(collective_id=0, has_side_effects=True),
    )(tokens, cotangent)


def parts_kernel(first, group, table_ref, tok_ref, cot_ref, *refs):
    gates, ups, downs = refs[:group], refs[group : 2 * group], refs[2 * group : 3 * group]
    out_ref = refs[3 * group]
    row, step = pl.program_id(0) + first, pl.program_id(1)
    tok, cot = tok_ref[...], cot_ref[...]
    for at in range(group):
        live = table_ref[row, step * group + at] >= 0
        rows = slice(at * ROWBLK, (at + 1) * ROWBLK)
        both = jnp.dot(
            tok,
            jnp.concatenate([gates[at][...], ups[at][...]], axis=1),
            preferred_element_type=jnp.float32,
        )
        grad = lax.dot_general(
            cot, downs[at][...], (((1,), (1,)), ((), ())), preferred_element_type=jnp.float32
        )
        out_ref[0, rows, :] = both[:, :BLK]
        out_ref[1, rows, :] = jnp.where(live, both[:, BLK:], 0.0)
        out_ref[2, rows, :] = jnp.where(live, grad, 0.0)


def weight_specs(first, group, feats):
    def block(table, row, step, at):
        return jnp.maximum(table[row + first, step * group + at], 0)

    def columns(at):
        return pl.BlockSpec((feats, BLK), lambda row, step, table: (0, block(table, row, step, at)))

    def rows(at):
        return pl.BlockSpec((BLK, feats), lambda row, step, table: (block(table, row, step, at), 0))

    return (
        [columns(at) for at in range(group)] * 2 + [rows(at) for at in range(group)]
    )


def partial_products(table, first, capacity, tok, cot, gate_w, up_w, down_w):
    row_blocks, feats = tok.shape[0] // ROWBLK, tok.shape[1]
    group = group_of(capacity)
    steps = capacity // group
    rows_spec = pl.BlockSpec((ROWBLK, feats), lambda row, step, table: (row, 0))
    flops = 6 * row_blocks * ROWBLK * feats * capacity * BLK
    return pl.pallas_call(
        functools.partial(parts_kernel, first, group),
        out_shape=jax.ShapeDtypeStruct((3, row_blocks * capacity * ROWBLK, BLK), jnp.float32),
        grid_spec=pltpu.PrefetchScalarGridSpec(
            num_scalar_prefetch=1,
            grid=(row_blocks, steps),
            in_specs=[rows_spec, rows_spec] + weight_specs(first, group, feats),
            out_specs=pl.BlockSpec(
                (3, group * ROWBLK, BLK), lambda row, step, table: (0, row * steps + step, 0)
            ),
        ),
        compiler_params=pltpu.CompilerParams(vmem_limit_bytes=PLAIN_LIMIT),
        cost_estimate=pl.CostEstimate(
            flops=flops, bytes_accessed=flops // ROWBLK, transcendentals=0
        ),
    )(table, tok, cot, *([gate_w] * group + [up_w] * group + [down_w] * group))


def exchange_kernel(
    count, inputs, *refs
):
    part_refs, all_ref = refs[:inputs], refs[inputs]
    (
        mine, paired, xsend, xland, zsend, zland, acts,
        load_sem, pair_send, pair_recv, x_send, x_recv, z_send, z_recv,
    up_send, down_send, side_send, all_recv, hand_send, hand_recv, own_sem,
    ) = refs[inputs + 1 :]
    _, _, subs, wide, tall, _, _ = part_refs[0].shape
    halves = inputs * subs
    chips = count // 2
    me = lax.axis_index("seq")
    chip, core = me // 2, lax.rem(me, 2)
    sibling = {"seq": me + 1 - 2 * core}
    along, across = chip // wide, lax.rem(chip, wide)
    order = sorted(range(1, tall), key=lambda shift: abs(2 * shift - tall))

    def device(i, j):
        return {"seq": (i * wide + j) * 2 + core}

    def column(shift):
        return lax.rem(across + shift, wide)

    def line(shift):
        return lax.rem(along + shift, tall)

    def remote(src, dst, send, recv, target):
        return pltpu.make_async_remote_copy(
            src_ref=src, dst_ref=dst, send_sem=send, recv_sem=recv,
            device_id=target, device_id_type=MESH,
        )

    barrier = pltpu.get_barrier_semaphore()
    pl.semaphore_signal(barrier, inc=1, device_id=sibling, device_id_type=MESH)
    for s in range(1, wide):
        pl.semaphore_signal(
            barrier, inc=1, device_id=device(along, column(s)), device_id_type=MESH
        )
    for d in range(1, tall):
        pl.semaphore_signal(barrier, inc=1, device_id=device(line(d), across), device_id_type=MESH)
    pl.semaphore_wait(barrier, wide + tall - 1)

    def part_at(h, s, d, side):
        return part_refs[h // subs].at[:, side, h % subs, column(s), line(d)]

    def load_copy(h, s, d):
        return pltpu.make_async_copy(
            part_at(h, s, d, core), mine.at[h, s, d], load_sem.at[h, s, d]
        )

    def pair_copy(h, s, d):
        return remote(
            part_at(h, s, d, 1 - core), paired.at[h, s, d],
            pair_send.at[h, s, d], pair_recv.at[h, s, d], sibling,
        )

    def x_copy(h, s, d):
        return remote(
            xsend.at[h, s - 1, d], xland.at[h, s - 1, d],
            x_send.at[h, s, d], x_recv.at[h, s, d], device(along, column(s)),
        )

    def z_copy(h, d):
        return remote(
            zsend.at[h, d - 1], zland.at[h, d - 1],
            z_send.at[h, d], z_recv.at[h, d], device(line(d), across),
        )

    def slot(h, i, j, side):
        return all_ref.at[h // subs, :, side, h % subs, j, i]

    def z_route(h, i, j, to, send, src=None):
        dst = slot(h, i, j, core)
        owner = i * wide + j
        return remote(
            dst if src is None else src, dst, send.at[h, owner], all_recv.at[h, owner],
            device(to, across),
        )

    def x_route(h, i, s, src=None):
        dst = slot(h, i, across, core)
        return remote(
            dst if src is None else src, dst, side_send.at[h, s, i],
            all_recv.at[h, i * wide + across], device(along, column(s)),
        )

    def hand_copy(h, i, j, side, src=None):
        dst = slot(h, i, j, side)
        owner = i * wide + j
        return remote(
            dst if src is None else src, dst, hand_send.at[h, owner], hand_recv.at[h, owner], sibling
        )

    def take(h, i, j):
        z_route(h, i, j, along, up_send).wait_recv()

    def pass_on(h, i, j, up, down, src=None):
        if up:

            @pl.when(along < tall - 1)
            def _():
                z_route(h, i, j, along + 1, up_send, src).start()

        if down:

            @pl.when(along > 0)
            def _():
                z_route(h, i, j, along - 1, down_send, src).start()

    def spread(h, i, src=None):
        for s in range(1, wide):
            x_route(h, i, s, src).start()

    for h in range(halves):
        for s in list(range(1, wide)) + [0]:
            for d in order + [0]:
                pair_copy(h, s, d).start()
                load_copy(h, s, d).start()

    for h in range(halves):
        for d in order + [0]:
            for s in range(1, wide):
                load_copy(h, s, d).wait()
                pair_copy(h, s, d).wait_recv()
                xsend[h, s - 1, d] = (mine[h, s, d] + paired[h, s, d]).astype(jnp.bfloat16)
                x_copy(h, s, d).start()

    def row_sum(h, d):
        load_copy(h, 0, d).wait()
        pair_copy(h, 0, d).wait_recv()
        total = mine[h, 0, d] + paired[h, 0, d]
        for s in range(1, wide):
            x_copy(h, s, d).wait_recv()
            total = total + xland[h, s - 1, d].astype(jnp.float32)
        return total

    for h in range(halves):
        for d in order:
            zsend[h, d - 1] = row_sum(h, d).astype(jnp.bfloat16)
            z_copy(h, d).start()

    def own_copy(h):
        return pltpu.make_async_copy(acts.at[h], slot(h, along, across, core), own_sem.at[h])

    for h in range(halves):
        total = row_sum(h, 0)
        for d in order:
            z_copy(h, d).wait_recv()
            total = total + zland[h, d - 1].astype(jnp.float32)
        gate, up, grad = total[0], total[1], total[2]
        sig = jax.nn.sigmoid(gate)
        acts[h, 0] = (gate * sig * up).astype(jnp.bfloat16)
        acts[h, 1] = (grad * up * sig * (1.0 + gate * (1.0 - sig))).astype(jnp.bfloat16)
        acts[h, 2] = (grad * gate * sig).astype(jnp.bfloat16)
        src = acts.at[h]
        pass_on(h, along, across, True, True, src)
        spread(h, along, src)
        hand_copy(h, along, across, core, src).start()
        own_copy(h).start()

    for h in range(halves):
        if h % 2 == 1:
            for s in range(1, wide):
                take(h, along, column(s))
                pass_on(h, along, column(s), True, True)
                hand_copy(h, along, column(s), core).start()
    for far in range(1, tall):
        for h in range(halves):
            for s in range(wide if h % 2 == 1 else 1):
                for sign in (-1, 1):

                    @pl.when(along >= far if sign < 0 else along + far < tall)
                    def _(h=h, s=s, sign=sign):
                        i = along + sign * far
                        take(h, i, column(s))
                        pass_on(h, i, column(s), sign < 0, sign > 0)
                        if h % 2 == 0:
                            spread(h, i)
                        hand_copy(h, i, column(s), core).start()

    for h in range(0, halves, 2):
        for s in range(1, wide):
            for d in [0] + list(range(1, tall)):
                take(h, line(d), column(s))
                hand_copy(h, line(d), column(s), core).start()

    for h in range(halves):
        own_copy(h).wait()

        def finish(owner, carry, h=h):
            i, j = owner // wide, lax.rem(owner, wide)
            hand_copy(h, i, j, 1 - core).wait_recv()
            hand_copy(h, i, j, core).wait_send()
            mine = jnp.bool_(True) if h % 2 == 1 else j == across

            @pl.when(jnp.logical_and(mine, jnp.logical_and(i <= along, along < tall - 1)))
            def _():
                z_route(h, i, j, along + 1, up_send).wait_send()

            @pl.when(jnp.logical_and(mine, jnp.logical_and(i >= along, along > 0)))
            def _():
                z_route(h, i, j, along - 1, down_send).wait_send()

            return carry

        lax.fori_loop(0, chips, finish, 0)
        for s in range(1, wide):
            if h % 2 == 1:
                x_route(h, along, s).wait_send()
            else:
                for i in range(tall):
                    x_route(h, i, s).wait_send()
        for d in range(tall):
            for s in range(wide):
                pair_copy(h, s, d).wait_send()
                if s > 0:
                    x_copy(h, s, d).wait_send()
            if d > 0:
                z_copy(h, d).wait_send()


def exchange(parts, collective_id):
    count = lax.axis_size("seq")
    chips = count // 2
    tall = 4 if chips % 4 == 0 else chips
    wide = chips // tall
    inputs = len(parts)
    own = parts[0].shape[1] // count
    subs = 2 if inputs == 1 and own % 32 == 0 else 1
    halves = inputs * subs
    piece = own // subs
    shape = (3, 2, subs, wide, tall, piece, BLK)
    chunk = (3, piece, BLK)
    dma = pltpu.SemaphoreType.DMA
    anywhere = pl.BlockSpec(memory_space=pl.ANY)
    out = pl.pallas_call(
        functools.partial(exchange_kernel, count, inputs),
        out_shape=jax.ShapeDtypeStruct((inputs,) + shape, jnp.bfloat16),
        in_specs=[anywhere] * inputs,
        out_specs=anywhere,
        scratch_shapes=[
            pltpu.VMEM((halves, wide, tall) + chunk, jnp.float32),
            pltpu.VMEM((halves, wide, tall) + chunk, jnp.float32),
            pltpu.VMEM((halves, max(wide - 1, 1), tall) + chunk, jnp.bfloat16),
            pltpu.VMEM((halves, max(wide - 1, 1), tall) + chunk, jnp.bfloat16),
            pltpu.VMEM((halves, max(tall - 1, 1)) + chunk, jnp.bfloat16),
            pltpu.VMEM((halves, max(tall - 1, 1)) + chunk, jnp.bfloat16),
            pltpu.VMEM((halves,) + chunk, jnp.bfloat16),
            dma((halves, wide, tall)),
            dma((halves, wide, tall)),
            dma((halves, wide, tall)),
            dma((halves, wide, tall)),
            dma((halves, wide, tall)),
            dma((halves, tall)),
            dma((halves, tall)),
            dma((halves, chips)),
            dma((halves, chips)),
            dma((halves, wide, tall)),
            dma((halves, chips)),
            dma((halves, chips)),
            dma((halves, chips)),
            dma((halves,)),
        ],
        compiler_params=pltpu.CompilerParams(
            collective_id=collective_id, has_side_effects=True, vmem_limit_bytes=COMM_LIMIT
        ),
    )(*(part.reshape(shape) for part in parts))
    return out.reshape((inputs,) + parts[0].shape)


def rows_out_kernel(group, table_ref, act_ref, *refs):
    gates, ups, downs = refs[:group], refs[group : 2 * group], refs[2 * group : 3 * group]
    out_ref = refs[3 * group]
    step = pl.program_id(1)

    @pl.when(step == 0)
    def _():
        out_ref[...] = jnp.zeros_like(out_ref)

    out = jnp.zeros(out_ref.shape[2:], jnp.float32)
    grad = jnp.zeros(out_ref.shape[2:], jnp.float32)
    across = (((1,), (1,)), ((), ()))
    for at in range(group):
        rows = slice(at * ROWBLK, (at + 1) * ROWBLK)
        out += jnp.dot(act_ref[0, 0, rows, :], downs[at][...], preferred_element_type=jnp.float32)
        grad += lax.dot_general(
            jnp.concatenate([act_ref[0, 1, rows, :], act_ref[0, 2, rows, :]], axis=1),
            jnp.concatenate([gates[at][...], ups[at][...]], axis=1),
            across,
            preferred_element_type=jnp.float32,
        )
    out_ref[0, 0] += out
    out_ref[0, 1] += grad


def rows_out(table, first, row_blocks, capacity, acts, gate_w, up_w, down_w):
    feats = gate_w.shape[0]
    group = group_of(capacity)
    steps = capacity // group
    if acts.shape[0] == row_blocks:
        place = lambda row, step, table: (row, 0, step, 0)
    else:
        place = lambda row, step, table: (0, 0, row * steps + step, 0)
    flops = 6 * row_blocks * ROWBLK * feats * capacity * BLK
    return pl.pallas_call(
        functools.partial(rows_out_kernel, group),
        out_shape=jax.ShapeDtypeStruct((row_blocks, 2, ROWBLK, feats), jnp.float32),
        grid_spec=pltpu.PrefetchScalarGridSpec(
            num_scalar_prefetch=1,
            grid=(row_blocks, steps),
            in_specs=[pl.BlockSpec((1, 3, group * ROWBLK, BLK), place)]
            + weight_specs(first, group, feats),
            out_specs=pl.BlockSpec((1, 2, ROWBLK, feats), lambda row, step, table: (row, 0, 0, 0)),
        ),
        compiler_params=pltpu.CompilerParams(vmem_limit_bytes=PLAIN_LIMIT),
        cost_estimate=pl.CostEstimate(
            flops=flops, bytes_accessed=flops // ROWBLK, transcendentals=0
        ),
    )(table, acts, *([gate_w] * group + [up_w] * group + [down_w] * group))


def weights_out_kernel(first, capacity, scale, pieces, group, passing, table_ref, *refs):
    toks, cots, refs = refs[:pieces], refs[pieces : 2 * pieces], refs[2 * pieces :]
    flipped, cot_all, dense = refs[-3:]
    units, refs = refs[:-3], None
    passed = ()
    if passing:
        units, passed = units[:-2], units[-2:]
    gate_ref, up_ref, down_ref = units[-3:]
    units = units[:-3]
    step = pl.program_id(0)
    rows = flipped.shape[1]
    row_blocks = rows // ROWBLK
    each = rows // pieces

    @pl.when(step == 0)
    def _():
        for at in range(pieces):
            cut = slice(at * each, (at + 1) * each)
            flipped[:, cut] = toks[at][...].T
            cot_all[cut, :] = cots[at][...]
        for at, out in enumerate(passed):
            out[...] = units[-1][at]

    for at in range(group):
        for row in range(row_blocks):
            kept = table_ref[first + row, capacity + 1 + step * group + at] >= 0
            unit = units[at * row_blocks + row]
            for which in range(3):
                value = unit[0, which]
                dense[which, row * ROWBLK : (row + 1) * ROWBLK, at * BLK : (at + 1) * BLK] = (
                    jnp.where(kept, value, jnp.zeros_like(value))
                )
    tok = flipped[...]
    gate_ref[...] = jnp.dot(tok, dense[1], preferred_element_type=jnp.float32) * scale
    up_ref[...] = jnp.dot(tok, dense[2], preferred_element_type=jnp.float32) * scale
    down_ref[...] = (
        lax.dot_general(
            dense[0], cot_all[...], (((0,), (0,)), ((), ())), preferred_element_type=jnp.float32
        )
        * scale
    )


def weights_out(table, first, capacity, toks, cots, acts, scale, passing=None):
    blocks = table.shape[1] - capacity - 1
    feats = toks[0].shape[1]
    pieces = len(toks)
    rows = pieces * toks[0].shape[0]
    row_blocks = rows // ROWBLK
    group = wide_group(blocks)
    held = acts.shape[2] // ROWBLK
    whole = pl.BlockSpec(toks[0].shape, lambda step, table: (0, 0))
    wide = pl.BlockSpec((feats, group * BLK), lambda step, table: (0, step))
    hidden = blocks * BLK

    extra, extra_shapes, extra_in = (), (), []
    if passing is not None:
        extra = (passing,)
        extra_shapes = (jax.ShapeDtypeStruct(passing.shape[1:], passing.dtype),) * 2
        extra_in = [pl.BlockSpec(passing.shape, lambda step, table: (0, 0, 0))]

    def unit_spec(at, row):
        def place(step, table):
            unit = jnp.maximum(table[first + row, capacity + 1 + step * group + at], 0)
            unit = unit + row * capacity
            return (unit // held, 0, lax.rem(unit, held), 0)

        return pl.BlockSpec((1, 3, ROWBLK, BLK), place)

    return pl.pallas_call(
        functools.partial(
            weights_out_kernel, first, capacity, scale, pieces, group, passing is not None
        ),
        out_shape=(
            jax.ShapeDtypeStruct((feats, hidden), jnp.float32),
            jax.ShapeDtypeStruct((feats, hidden), jnp.float32),
            jax.ShapeDtypeStruct((hidden, feats), jnp.float32),
        )
        + extra_shapes,
        grid_spec=pltpu.PrefetchScalarGridSpec(
            num_scalar_prefetch=1,
            grid=(blocks // group,),
            in_specs=[whole] * (2 * pieces)
            + [unit_spec(at, row) for at in range(group) for row in range(row_blocks)]
            + extra_in,
            out_specs=(
                wide,
                wide,
                pl.BlockSpec((group * BLK, feats), lambda step, table: (step, 0)),
            )
            + (whole,) * len(extra_shapes),
            scratch_shapes=[
                pltpu.VMEM((feats, rows), jnp.bfloat16),
                pltpu.VMEM((rows, feats), jnp.bfloat16),
                pltpu.VMEM((3, rows, group * BLK), jnp.bfloat16),
            ],
        ),
        compiler_params=pltpu.CompilerParams(vmem_limit_bytes=WIDE_LIMIT),
        cost_estimate=pl.CostEstimate(
            flops=6 * rows * feats * hidden, bytes_accessed=12 * feats * hidden, transcendentals=0
        ),
    )(table, *toks, *cots, *([acts] * (group * row_blocks)), *extra)


def fused_kernel(mode, count, *refs):
    swapped, both = mode == "other", mode == "both"
    rows_held = 2 if both else 1
    moving = swapped or both
    table_ref, tok_ref, cot_ref, gate_hbm, up_hbm, down_hbm = refs[:6]
    refs = refs[6:]
    acts_out, tok_out, cot_out = refs[:3] if moving else (refs[0], None, None)
    refs = refs[3 if moving else 1 :]
    outs, refs = refs[:rows_held], refs[rows_held:]
    (
        gate_w, up_w, down_w, toks, cots, parts, paired, xsend, xland, zsend, zland, acts,
        sums, weight_sem, row_load, row_send, row_recv, row_store, pair_send, pair_recv, x_send, x_recv,
        z_send, z_recv, up_send, down_send, side_send, all_recv, hand_send, hand_recv, out_sem,
    ) = refs
    groups, _, held, _ = parts.shape
    rows = toks.shape[0]
    first = 1 if swapped else 0
    units = held // ROWBLK
    _, wide, tall, _, piece, _ = paired.shape
    chips = count // 2
    me, rank = lax.axis_index("seq"), lax.axis_index("tp")
    chip, core = me // 2, lax.rem(me, 2)
    sibling, partner = {"seq": me + 1 - 2 * core}, {"tp": 1 - rank}
    along, across = chip // wide, lax.rem(chip, wide)
    order = sorted(range(1, tall), key=lambda shift: abs(2 * shift - tall))
    contract = (((1,), (1,)), ((), ()))

    def device(i, j):
        return {"seq": (i * wide + j) * 2 + core}

    def column(shift):
        return lax.rem(across + shift, wide)

    def line(shift):
        return lax.rem(along + shift, tall)

    def rows_of(side, i, j):
        return pl.ds(pl.multiple_of(((side * wide + j) * tall + i) * piece, 16), piece)

    def remote(src, dst, send, recv, target):
        return pltpu.make_async_remote_copy(
            src_ref=src, dst_ref=dst, send_sem=send, recv_sem=recv,
            device_id=target, device_id_type=MESH,
        )

    def signal(target):
        pl.semaphore_signal(
            pltpu.get_barrier_semaphore(), inc=1, device_id=target, device_id_type=MESH
        )

    blocks = down_w.shape[0]
    own_rows = [
        pltpu.make_async_copy(src, dst.at[0], row_load.at[at])
        for at, (src, dst) in enumerate(((tok_ref, toks), (cot_ref, cots)))
        if not swapped
    ]

    def start_columns(block, carry):
        cut = pl.ds(pl.multiple_of(block * BLK, BLK), BLK)
        pltpu.make_async_copy(gate_hbm.at[:, cut], gate_w.at[block], weight_sem.at[0]).start()
        pltpu.make_async_copy(up_hbm.at[:, cut], up_w.at[block], weight_sem.at[1]).start()
        return carry

    def start_lines(block, carry):
        cut = pl.ds(pl.multiple_of(block * BLK, BLK), BLK)
        pltpu.make_async_copy(down_hbm.at[cut, :], down_w.at[block], weight_sem.at[2]).start()
        return carry

    for copy in own_rows:
        copy.start()
    lax.fori_loop(0, blocks, start_columns, 0)
    lax.fori_loop(0, blocks, start_lines, 0)

    signal(sibling)
    for s in range(1, wide):
        signal(device(along, column(s)))
    for d in range(1, tall):
        signal(device(line(d), across))
    if moving:
        signal(partner)
    pl.semaphore_wait(pltpu.get_barrier_semaphore(), wide + tall - 1 + (1 if moving else 0))

    row_copies = [
        remote(src, dst.at[rows - 1], row_send.at[at], row_recv.at[at], partner)
        for at, (src, dst) in enumerate(((tok_ref, toks), (cot_ref, cots)))
        if moving
    ]
    for copy in row_copies:
        copy.start()
    row_stores = [
        pltpu.make_async_copy(src.at[rows - 1], dst, row_store.at[at])
        for at, (src, dst) in enumerate(((toks, tok_out), (cots, cot_out)))
        if moving
    ]

    def pair_copy(h, s, d):
        return remote(
            parts.at[h, :, rows_of(1 - core, line(d), column(s))], paired.at[h, s, d],
            pair_send.at[h, s, d], pair_recv.at[h, s, d], sibling,
        )

    def x_copy(h, s, d):
        return remote(
            xsend.at[h, s - 1, d], xland.at[h, s - 1, d],
            x_send.at[h, s, d], x_recv.at[h, s, d], device(along, column(s)),
        )

    def z_copy(h, d):
        return remote(
            zsend.at[h, d - 1], zland.at[h, d - 1],
            z_send.at[h, d], z_recv.at[h, d], device(line(d), across),
        )

    def slot(h, i, j, side):
        return acts.at[h, :, rows_of(side, i, j)]

    def z_route(h, i, j, to, send):
        dst, owner = slot(h, i, j, core), i * wide + j
        return remote(
            dst, dst, send.at[h, owner], all_recv.at[h, owner], device(to, across)
        )

    def x_route(h, i, s):
        dst = slot(h, i, across, core)
        return remote(
            dst, dst, side_send.at[h, s, i], all_recv.at[h, i * wide + across],
            device(along, column(s)),
        )

    def hand_copy(h, i, j, side):
        dst, owner = slot(h, i, j, side), i * wide + j
        return remote(dst, dst, hand_send.at[h, owner], hand_recv.at[h, owner], sibling)

    def out_copy(h):
        return pltpu.make_async_copy(acts.at[h], acts_out.at[h], out_sem.at[h])

    def take(h, i, j):
        z_route(h, i, j, along, up_send).wait_recv()

    def pass_on(h, i, j, up, down):
        if up:

            @pl.when(along < tall - 1)
            def _():
                z_route(h, i, j, along + 1, up_send).start()

        if down:

            @pl.when(along > 0)
            def _():
                z_route(h, i, j, along - 1, down_send).start()

    def spread(h, i):
        for s in range(1, wide):
            x_route(h, i, s).start()

    def line_first(h):
        return True

    def row_of(h):
        return h * rows // groups

    def block_of(h, unit):
        base = h % (groups // rows) * units
        return table_ref[first + row_of(h), base + unit]

    def unit_rows(unit):
        return pl.ds(pl.multiple_of(unit * ROWBLK, ROWBLK), ROWBLK)

    begin = (1 - core) * (units // 2 // 2)

    def column_step(h, pair):
        tok = toks[row_of(h)]
        for one in range(2):
            block, at = block_of(h, 2 * pair + one), unit_rows(2 * pair + one)
            value = jnp.dot(
                tok,
                jnp.concatenate([gate_w[block], up_w[block]], axis=1),
                preferred_element_type=jnp.float32,
            )
            parts[h, 0, at, :] = value[:, :BLK]
            parts[h, 1, at, :] = value[:, BLK:]

    def line_step(h, pair):
        grad = lax.dot_general(
            cots[row_of(h)],
            jnp.concatenate(
                [down_w[block_of(h, 2 * pair)], down_w[block_of(h, 2 * pair + 1)]], axis=0
            ),
            contract,
            preferred_element_type=jnp.float32,
        )
        parts[h, 2, unit_rows(2 * pair), :] = grad[:, :BLK]
        parts[h, 2, unit_rows(2 * pair + 1), :] = grad[:, BLK:]

    def each_pair(h, low, high, *steps):
        def body(turn, carry):
            for step in steps:
                step(h, lax.rem(turn + begin, units // 2))
            return carry

        lax.fori_loop(low, high, body, 0)

    def columns_times(h, low, high):
        each_pair(h, low, high, column_step)

    def lines_times(h, low, high):
        each_pair(h, low, high, line_step)

    def multiply(h, low, high):
        each_pair(h, low, high, column_step, line_step)

    def pair_stage(h):
        for s in list(range(1, wide)) + [0]:
            for d in order + [0]:
                pair_copy(h, s, d).start()

    def x_stage(h):
        for d in order + [0]:
            for s in range(1, wide):
                pair_copy(h, s, d).wait_recv()
                xsend[h, s - 1, d] = (
                    parts[h, :, rows_of(core, line(d), column(s)), :] + paired[h, s, d]
                ).astype(jnp.bfloat16)
                x_copy(h, s, d).start()

    def row_sum(h, d):
        pair_copy(h, 0, d).wait_recv()
        total = parts[h, :, rows_of(core, line(d), across), :] + paired[h, 0, d]
        for s in range(1, wide):
            x_copy(h, s, d).wait_recv()
            total = total + xland[h, s - 1, d].astype(jnp.float32)
        return total

    def z_piece(h, at):
        d = order[at]
        zsend[h, d - 1] = row_sum(h, d).astype(jnp.bfloat16)
        z_copy(h, d).start()

    def z_stage(h):
        for at in range(len(order)):
            z_piece(h, at)

    def act_stage(h):
        total = row_sum(h, 0)
        for d in order:
            z_copy(h, d).wait_recv()
            total = total + zland[h, d - 1].astype(jnp.float32)
        gate, up, grad = total[0], total[1], total[2]
        sig = jax.nn.sigmoid(gate)
        own = rows_of(core, along, across)
        acts[h, 0, own, :] = (gate * sig * up).astype(jnp.bfloat16)
        acts[h, 1, own, :] = (grad * up * sig * (1.0 + gate * (1.0 - sig))).astype(jnp.bfloat16)
        acts[h, 2, own, :] = (grad * gate * sig).astype(jnp.bfloat16)
        pass_on(h, along, across, True, True)
        spread(h, along)
        hand_copy(h, along, across, core).start()

    def gather_stage(h, far):
        if far == 1 and not line_first(h):
            for s in range(1, wide):
                take(h, along, column(s))
                pass_on(h, along, column(s), True, True)
                hand_copy(h, along, column(s), core).start()
        for s in range(1 if line_first(h) else wide):
            for sign in (-1, 1):

                @pl.when(along >= far if sign < 0 else along + far < tall)
                def _(s=s, sign=sign):
                    i = along + sign * far
                    take(h, i, column(s))
                    pass_on(h, i, column(s), sign < 0, sign > 0)
                    if line_first(h):
                        spread(h, i)
                    hand_copy(h, i, column(s), core).start()

    def side_stage(h):
        if line_first(h):
            for s in range(1, wide):
                for d in range(tall):
                    take(h, line(d), column(s))
                    hand_copy(h, line(d), column(s), core).start()

    def sums_stage(h):
        def arrive(owner, carry):
            hand_copy(h, owner // wide, lax.rem(owner, wide), 1 - core).wait_recv()
            return carry

        lax.fori_loop(0, chips, arrive, 0)
        out_copy(h).start()
        row = row_of(h)

        def step(pair, carry):
            at = (unit_rows(2 * pair), unit_rows(2 * pair + 1))
            cut = (block_of(h, 2 * pair), block_of(h, 2 * pair + 1))
            sums[row, 0] += jnp.dot(
                jnp.concatenate([acts[h, 0, at[0], :], acts[h, 0, at[1], :]], axis=1),
                jnp.concatenate([down_w[cut[0]], down_w[cut[1]]], axis=0),
                preferred_element_type=jnp.float32,
            )
            grad = sums[row, 1]
            for one in range(2):
                grad += lax.dot_general(
                    jnp.concatenate([acts[h, 1, at[one], :], acts[h, 2, at[one], :]], axis=1),
                    jnp.concatenate([gate_w[cut[one]], up_w[cut[one]]], axis=1),
                    contract,
                    preferred_element_type=jnp.float32,
                )
            sums[row, 1] = grad
            return carry

        lax.fori_loop(0, units // 2, step, 0)

    sums[...] = jnp.zeros_like(sums)
    for copy in own_rows:
        copy.wait()
    half = (units // 2 + 1) // 2

    def weights_arrive(at, held_w):
        pltpu.make_async_copy(held_w, held_w, weight_sem.at[at]).wait()

    pairs = units // 2
    early = groups > 2
    for h in range(groups):
        crossing = moving and h == (0 if swapped else groups // 2)
        if h == 0:
            weights_arrive(0, gate_w)
            weights_arrive(1, up_w)
        if crossing:
            row_copies[0].wait_recv()
        columns_times(h, 0, half)
        if h == 0:
            weights_arrive(2, down_w)
        if crossing:
            row_copies[1].wait_recv()
            for copy in row_stores:
                copy.start()
        lines_times(h, 0, half)
        pair_stage(h)
        multiply(h, half, pairs)
        if h > 0:
            for at in range(len(order) - 1):
                z_piece(h - 1, at)
        x_stage(h)
        if h > 0:
            z_piece(h - 1, len(order) - 1)
        if early and h == groups - 1:
            act_stage(0)
    last = tall + 1
    for turn in range(groups + last):
        if turn == groups - 2:
            z_stage(groups - 1)
        for h in range(groups):
            at = turn - h
            if 1 <= at < tall:
                gather_stage(h, at)
            elif at == tall:
                side_stage(h)
            elif at == 0 and not (early and h == 0):
                act_stage(h)
        if 0 <= turn - last < groups:
            sums_stage(turn - last)

    alive = table_ref[first + rows - 1, table_ref.shape[1] - 1].astype(jnp.float32)
    for row, out in enumerate(outs):
        value = sums[row]
        if both:
            value = value * alive
        out[...] = value.astype(out.dtype)

    for h in range(groups):

        def finish(owner, carry, h=h):
            i, j = owner // wide, lax.rem(owner, wide)
            hand_copy(h, i, j, core).wait_send()
            mine = j == across if line_first(h) else jnp.bool_(True)

            @pl.when(jnp.logical_and(mine, jnp.logical_and(i <= along, along < tall - 1)))
            def _():
                z_route(h, i, j, along + 1, up_send).wait_send()

            @pl.when(jnp.logical_and(mine, jnp.logical_and(i >= along, along > 0)))
            def _():
                z_route(h, i, j, along - 1, down_send).wait_send()

            return carry

        lax.fori_loop(0, chips, finish, 0)
        for s in range(1, wide):
            if line_first(h):
                for i in range(tall):
                    x_route(h, i, s).wait_send()
            else:
                x_route(h, along, s).wait_send()
        for d in range(tall):
            for s in range(wide):
                pair_copy(h, s, d).wait_send()
                if s > 0:
                    x_copy(h, s, d).wait_send()
            if d > 0:
                z_copy(h, d).wait_send()
        out_copy(h).wait()
    for copy in row_copies:
        copy.wait_send()
    for copy in row_stores:
        copy.wait()


def fused(mode, table, capacity, tok, cot, gate_w, up_w, down_w, collective_id):
    count = lax.axis_size("seq")
    chips = count // 2
    tall = 4 if chips % 4 == 0 else chips
    wide = chips // tall
    rows = 2 if mode == "both" else 1
    groups = 2 * rows
    feats, blocks = gate_w.shape[0], gate_w.shape[1] // BLK
    held = capacity // 2 * ROWBLK
    piece = held // count
    chunk = (3, piece, BLK)
    dma = pltpu.SemaphoreType.DMA
    anywhere = pl.BlockSpec(memory_space=pl.ANY)
    out_shape = [jax.ShapeDtypeStruct((groups, 3, held, BLK), jnp.bfloat16)]
    out_specs = [anywhere]
    if mode != "own":
        out_shape += [jax.ShapeDtypeStruct(tok.shape, tok.dtype)] * 2
        out_specs += [anywhere] * 2
    if mode == "both":
        out_shape += [jax.ShapeDtypeStruct((2,) + tok.shape, jnp.float32)]
    out_shape += [jax.ShapeDtypeStruct((2,) + tok.shape, jnp.bfloat16)]
    out_specs += [pl.BlockSpec(memory_space=pltpu.VMEM)] * rows
    flops = 12 * rows * ROWBLK * tok.shape[1] * capacity * BLK
    return pl.pallas_call(
        functools.partial(fused_kernel, mode, count),
        out_shape=tuple(out_shape),
        in_specs=[pl.BlockSpec(memory_space=pltpu.SMEM)] + [anywhere] * 5,
        out_specs=tuple(out_specs),
        scratch_shapes=[
            pltpu.VMEM((blocks, feats, BLK), gate_w.dtype),
            pltpu.VMEM((blocks, feats, BLK), up_w.dtype),
            pltpu.VMEM((blocks, BLK, feats), down_w.dtype),
            pltpu.VMEM((rows,) + tok.shape, tok.dtype),
            pltpu.VMEM((rows,) + tok.shape, tok.dtype),
            pltpu.VMEM((groups, 3, held, BLK), jnp.float32),
            pltpu.VMEM((groups, wide, tall) + chunk, jnp.float32),
            pltpu.VMEM((groups, wide - 1, tall) + chunk, jnp.bfloat16),
            pltpu.VMEM((groups, wide - 1, tall) + chunk, jnp.bfloat16),
            pltpu.VMEM((groups, tall - 1) + chunk, jnp.bfloat16),
            pltpu.VMEM((groups, tall - 1) + chunk, jnp.bfloat16),
            pltpu.VMEM((groups, 3, held, BLK), jnp.bfloat16),
            pltpu.VMEM((rows, 2) + tok.shape, jnp.float32),
            dma((3,)),
            dma((2,)),
            dma((2,)),
            dma((2,)),
            dma((2,)),
            dma((groups, wide, tall)),
            dma((groups, wide, tall)),
            dma((groups, wide, tall)),
            dma((groups, wide, tall)),
            dma((groups, tall)),
            dma((groups, tall)),
            dma((groups, chips)),
            dma((groups, chips)),
            dma((groups, wide, tall)),
            dma((groups, chips)),
            dma((groups, chips)),
            dma((groups, chips)),
            dma((groups,)),
        ],
        compiler_params=pltpu.CompilerParams(
            collective_id=collective_id, has_side_effects=True, vmem_limit_bytes=FUSED_LIMIT
        ),
        cost_estimate=pl.CostEstimate(
            flops=flops, bytes_accessed=6 * gate_w.size, transcendentals=0
        ),
    )(table, tok, cot, gate_w, up_w, down_w)


def shards(tokens, gate_weight, up_weight, down_weight, masks, cotangent):
    tp_count = lax.axis_size("tp")
    seq_count = lax.axis_size("seq")
    rank = lax.axis_index("tp")
    rows, feats = tokens.shape
    total_rows = rows * tp_count
    row_blocks, blocks = masks.shape
    kept_total = blocks * tp_count // KEEP_PART
    capacity = min(2 * kept_total // tp_count, blocks)
    scale = 1.0 / math.sqrt(total_rows)
    weights = (gate_weight, up_weight, down_weight)

    fits = seq_count % 8 == 0 and capacity % 4 == 0 and capacity // 2 * ROWBLK % (16 * seq_count) == 0
    if tp_count != 2 or row_blocks != 2 or rows != ROWBLK or not fits:
        table, _, _ = unit_tables(masks, jnp.int32(0), capacity)
        tok, cot = (value.reshape(total_rows, feats) for value in gather_rows(tokens, cotangent))
        parts = partial_products(table, 0, capacity, tok, cot, *weights)
        acts = exchange([parts], 1)
        row_parts = rows_out(table, 0, row_blocks, capacity, acts, *weights)
        row_parts = jnp.swapaxes(row_parts.reshape(tp_count, rows // ROWBLK, 2, ROWBLK, feats), 1, 2)
        moved = []
        for shift in range(1, tp_count):
            piece = lax.dynamic_index_in_dim(
                row_parts, lax.rem(rank + shift, tp_count), 0, keepdims=False
            ).astype(jnp.bfloat16)
            pairs = [(src, (src + shift) % tp_count) for src in range(tp_count)]
            moved.append(lax.ppermute(piece, "tp", pairs))
        grads = weights_out(table, 0, capacity, [tok], [cot], acts, scale)
        mine = lax.dynamic_index_in_dim(row_parts, rank, 0, keepdims=False)
        for piece in moved:
            mine = mine + piece.astype(jnp.float32)
        mine = mine.reshape(2, rows, feats).astype(jnp.bfloat16)
        return (mine[0], mine[1]) + tuple(grads)

    table, index, case = unit_tables(masks, rank, capacity)

    def swap(value):
        return lax.ppermute(value, "tp", [(0, 1), (1, 0)])

    def one_row(own, _):
        first = 0 if own else 1
        acts, *rest = fused(
            "own" if own else "other", index, capacity, tokens, cotangent, *weights, 2 + first
        )
        if own:
            grads = weights_out(table, 0, capacity, [tokens], [cotangent], acts, scale, rest[0])
            return tuple(grads[3:]) + tuple(grads[:3])
        tok, cot, sums = rest
        sums = swap(sums)
        grads = weights_out(table, 1, capacity, [tok], [cot], acts, scale)
        return (sums[0], sums[1]) + tuple(grads)

    def both_rows(_):
        acts, tok, cot, mine, other = fused(
            "both", index, capacity, tokens, cotangent, *weights, 1
        )
        moved = swap(other)
        grads = weights_out(table, 0, capacity, [tokens, tok], [cotangent, cot], acts, scale)
        total = (mine + moved.astype(jnp.float32)).astype(jnp.bfloat16)
        return (total[0], total[1]) + tuple(grads)

    return lax.switch(
        case[0],
        [functools.partial(one_row, True), functools.partial(one_row, False), both_rows],
        None,
    )


def solution(mesh):
    placed = (
        P("tp", "seq"),
        P("seq", "tp"),
        P("seq", "tp"),
        P("tp", "seq"),
        P(None, "tp"),
        P("tp", "seq"),
    )
    return jax.shard_map(
        shards,
        mesh=mesh,
        in_specs=placed,
        out_specs=(P("tp", "seq"), P("tp", "seq"), P("seq", "tp"), P("seq", "tp"), P("tp", "seq")),
        check_vma=False,
    )
```

```python
import functools
import math

import jax
import jax.numpy as jnp
from jax import lax
from jax.experimental import pallas as pl
from jax.experimental.pallas import tpu as pltpu
from jax.sharding import PartitionSpec as P

BLK = 128
ROWBLK = 128
KEEP_PART = 4
MESH = pl.DeviceIdType.MESH
PLAIN_LIMIT = 20 * 1024 * 1024
COMM_LIMIT = 28 * 1024 * 1024
WIDE_LIMIT = 32 * 1024 * 1024
FUSED_LIMIT = 60 * 1024 * 1024


def group_of(count):
    for size in (7, 8, 4, 2):
        if count % size == 0:
            return size
    return 1


def wide_group(count):
    for size in (7, 8, 4, 2):
        if count % size == 0:
            return size
    return 1


def tables_kernel(capacity, first_ref, mask_ref, table_ref, index_ref, case_ref):
    row_blocks, blocks = mask_ref.shape
    sources = [lax.rem(first_ref[0] + row, row_blocks) for row in range(row_blocks)]

    def clear(slot, carry):
        for row in range(row_blocks):
            table_ref[row, slot] = -1
            index_ref[row, slot] = 0
        return carry

    lax.fori_loop(0, capacity + 1, clear, 0, unroll=True)

    def step(block, taken):
        following = []
        for row in range(row_blocks):
            kept = mask_ref[sources[row], block]
            at = jnp.minimum(taken[row], capacity)
            table_ref[row, at] = jnp.where(kept == 1, block, -1)
            index_ref[row, at] = jnp.where(kept == 1, block, 0)
            table_ref[row, capacity + 1 + block] = jnp.where(kept == 1, at, -1)
            following.append(taken[row] + kept)
        return tuple(following)

    counts = lax.fori_loop(0, blocks, step, (jnp.int32(0),) * row_blocks, unroll=8)
    for row in range(row_blocks):
        index_ref[row, capacity] = jnp.minimum(counts[row], 1)
    mine, other = counts[0] > 0, counts[row_blocks - 1] > 0
    case_ref[0] = jnp.where(mine == other, 2, jnp.where(mine, 0, 1))


def unit_tables(masks, first, capacity):
    row_blocks, blocks = masks.shape
    smem = pl.BlockSpec(memory_space=pltpu.SMEM)
    return pl.pallas_call(
        functools.partial(tables_kernel, capacity),
        out_shape=(
            jax.ShapeDtypeStruct((row_blocks, capacity + 1 + blocks), jnp.int32),
            jax.ShapeDtypeStruct((row_blocks, capacity + 1), jnp.int32),
            jax.ShapeDtypeStruct((1,), jnp.int32),
        ),
        in_specs=[smem, smem],
        out_specs=(smem, smem, smem),
    )(first.reshape(1), masks)


def rows_kernel(count, tok_ref, cot_ref, tok_all, cot_all, send_sem, recv_sem, own_sem):
    me = lax.axis_index("tp")
    barrier = pltpu.get_barrier_semaphore()
    for shift in range(1, count):
        pl.semaphore_signal(
            barrier, inc=1, device_id={"tp": lax.rem(me + shift, count)}, device_id_type=MESH
        )
    pl.semaphore_wait(barrier, count - 1)
    copies = []
    for which, (src, dst) in enumerate(((tok_ref, tok_all), (cot_ref, cot_all))):
        for shift in range(1, count):
            copy = pltpu.make_async_remote_copy(
                src_ref=src,
                dst_ref=dst.at[me],
                send_sem=send_sem.at[which, shift],
                recv_sem=recv_sem.at[which, shift],
                device_id={"tp": lax.rem(me + shift, count)},
                device_id_type=MESH,
            )
            copy.start()
            copies.append(copy)
        own = pltpu.make_async_copy(src, dst.at[me], own_sem.at[which])
        own.start()
        copies.append(own)
    for copy in copies:
        copy.wait()


def gather_rows(tokens, cotangent):
    count = lax.axis_size("tp")
    rows, feats = tokens.shape
    anywhere = pl.BlockSpec(memory_space=pl.ANY)
    return pl.pallas_call(
        functools.partial(rows_kernel, count),
        out_shape=(jax.ShapeDtypeStruct((count, rows, feats), tokens.dtype),) * 2,
        in_specs=[anywhere] * 2,
        out_specs=(anywhere,) * 2,
        scratch_shapes=[
            pltpu.SemaphoreType.DMA((2, count)),
            pltpu.SemaphoreType.DMA((2, count)),
            pltpu.SemaphoreType.DMA((2,)),
        ],
        compiler_params=pltpu.CompilerParams(collective_id=0, has_side_effects=True),
    )(tokens, cotangent)


def parts_kernel(first, group, table_ref, tok_ref, cot_ref, *refs):
    gates, ups, downs = refs[:group], refs[group : 2 * group], refs[2 * group : 3 * group]
    out_ref = refs[3 * group]
    row, step = pl.program_id(0) + first, pl.program_id(1)
    tok, cot = tok_ref[...], cot_ref[...]
    for at in range(group):
        live = table_ref[row, step * group + at] >= 0
        rows = slice(at * ROWBLK, (at + 1) * ROWBLK)
        both = jnp.dot(
            tok,
            jnp.concatenate([gates[at][...], ups[at][...]], axis=1),
            preferred_element_type=jnp.float32,
        )
        grad = lax.dot_general(
            cot, downs[at][...], (((1,), (1,)), ((), ())), preferred_element_type=jnp.float32
        )
        out_ref[0, rows, :] = both[:, :BLK]
        out_ref[1, rows, :] = jnp.where(live, both[:, BLK:], 0.0)
        out_ref[2, rows, :] = jnp.where(live, grad, 0.0)


def weight_specs(first, group, feats):
    def block(table, row, step, at):
        return jnp.maximum(table[row + first, step * group + at], 0)

    def columns(at):
        return pl.BlockSpec((feats, BLK), lambda row, step, table: (0, block(table, row, step, at)))

    def rows(at):
        return pl.BlockSpec((BLK, feats), lambda row, step, table: (block(table, row, step, at), 0))

    return (
        [columns(at) for at in range(group)] * 2 + [rows(at) for at in range(group)]
    )


def partial_products(table, first, capacity, tok, cot, gate_w, up_w, down_w):
    row_blocks, feats = tok.shape[0] // ROWBLK, tok.shape[1]
    group = group_of(capacity)
    steps = capacity // group
    rows_spec = pl.BlockSpec((ROWBLK, feats), lambda row, step, table: (row, 0))
    flops = 6 * row_blocks * ROWBLK * feats * capacity * BLK
    return pl.pallas_call(
        functools.partial(parts_kernel, first, group),
        out_shape=jax.ShapeDtypeStruct((3, row_blocks * capacity * ROWBLK, BLK), jnp.float32),
        grid_spec=pltpu.PrefetchScalarGridSpec(
            num_scalar_prefetch=1,
            grid=(row_blocks, steps),
            in_specs=[rows_spec, rows_spec] + weight_specs(first, group, feats),
            out_specs=pl.BlockSpec(
                (3, group * ROWBLK, BLK), lambda row, step, table: (0, row * steps + step, 0)
            ),
        ),
        compiler_params=pltpu.CompilerParams(vmem_limit_bytes=PLAIN_LIMIT),
        cost_estimate=pl.CostEstimate(
            flops=flops, bytes_accessed=flops // ROWBLK, transcendentals=0
        ),
    )(table, tok, cot, *([gate_w] * group + [up_w] * group + [down_w] * group))


def exchange_kernel(
    count, inputs, *refs
):
    part_refs, all_ref = refs[:inputs], refs[inputs]
    (
        mine, paired, xsend, xland, zsend, zland, acts,
        load_sem, pair_send, pair_recv, x_send, x_recv, z_send, z_recv,
    up_send, down_send, side_send, all_recv, hand_send, hand_recv, own_sem,
    ) = refs[inputs + 1 :]
    _, _, subs, wide, tall, _, _ = part_refs[0].shape
    halves = inputs * subs
    chips = count // 2
    me = lax.axis_index("seq")
    chip, core = me // 2, lax.rem(me, 2)
    sibling = {"seq": me + 1 - 2 * core}
    along, across = chip // wide, lax.rem(chip, wide)
    order = sorted(range(1, tall), key=lambda shift: abs(2 * shift - tall))

    def device(i, j):
        return {"seq": (i * wide + j) * 2 + core}

    def column(shift):
        return lax.rem(across + shift, wide)

    def line(shift):
        return lax.rem(along + shift, tall)

    def remote(src, dst, send, recv, target):
        return pltpu.make_async_remote_copy(
            src_ref=src, dst_ref=dst, send_sem=send, recv_sem=recv,
            device_id=target, device_id_type=MESH,
        )

    barrier = pltpu.get_barrier_semaphore()
    pl.semaphore_signal(barrier, inc=1, device_id=sibling, device_id_type=MESH)
    for s in range(1, wide):
        pl.semaphore_signal(
            barrier, inc=1, device_id=device(along, column(s)), device_id_type=MESH
        )
    for d in range(1, tall):
        pl.semaphore_signal(barrier, inc=1, device_id=device(line(d), across), device_id_type=MESH)
    pl.semaphore_wait(barrier, wide + tall - 1)

    def part_at(h, s, d, side):
        return part_refs[h // subs].at[:, side, h % subs, column(s), line(d)]

    def load_copy(h, s, d):
        return pltpu.make_async_copy(
            part_at(h, s, d, core), mine.at[h, s, d], load_sem.at[h, s, d]
        )

    def pair_copy(h, s, d):
        return remote(
            part_at(h, s, d, 1 - core), paired.at[h, s, d],
            pair_send.at[h, s, d], pair_recv.at[h, s, d], sibling,
        )

    def x_copy(h, s, d):
        return remote(
            xsend.at[h, s - 1, d], xland.at[h, s - 1, d],
            x_send.at[h, s, d], x_recv.at[h, s, d], device(along, column(s)),
        )

    def z_copy(h, d):
        return remote(
            zsend.at[h, d - 1], zland.at[h, d - 1],
            z_send.at[h, d], z_recv.at[h, d], device(line(d), across),
        )

    def slot(h, i, j, side):
        return all_ref.at[h // subs, :, side, h % subs, j, i]

    def z_route(h, i, j, to, send, src=None):
        dst = slot(h, i, j, core)
        owner = i * wide + j
        return remote(
            dst if src is None else src, dst, send.at[h, owner], all_recv.at[h, owner],
            device(to, across),
        )

    def x_route(h, i, s, src=None):
        dst = slot(h, i, across, core)
        return remote(
            dst if src is None else src, dst, side_send.at[h, s, i],
            all_recv.at[h, i * wide + across], device(along, column(s)),
        )

    def hand_copy(h, i, j, side, src=None):
        dst = slot(h, i, j, side)
        owner = i * wide + j
        return remote(
            dst if src is None else src, dst, hand_send.at[h, owner], hand_recv.at[h, owner], sibling
        )

    def take(h, i, j):
        z_route(h, i, j, along, up_send).wait_recv()

    def pass_on(h, i, j, up, down, src=None):
        if up:

            @pl.when(along < tall - 1)
            def _():
                z_route(h, i, j, along + 1, up_send, src).start()

        if down:

            @pl.when(along > 0)
            def _():
                z_route(h, i, j, along - 1, down_send, src).start()

    def spread(h, i, src=None):
        for s in range(1, wide):
            x_route(h, i, s, src).start()

    for h in range(halves):
        for s in list(range(1, wide)) + [0]:
            for d in order + [0]:
                pair_copy(h, s, d).start()
                load_copy(h, s, d).start()

    for h in range(halves):
        for d in order + [0]:
            for s in range(1, wide):
                load_copy(h, s, d).wait()
                pair_copy(h, s, d).wait_recv()
                xsend[h, s - 1, d] = (mine[h, s, d] + paired[h, s, d]).astype(jnp.bfloat16)
                x_copy(h, s, d).start()

    def row_sum(h, d):
        load_copy(h, 0, d).wait()
        pair_copy(h, 0, d).wait_recv()
        total = mine[h, 0, d] + paired[h, 0, d]
        for s in range(1, wide):
            x_copy(h, s, d).wait_recv()
            total = total + xland[h, s - 1, d].astype(jnp.float32)
        return total

    for h in range(halves):
        for d in order:
            zsend[h, d - 1] = row_sum(h, d).astype(jnp.bfloat16)
            z_copy(h, d).start()

    def own_copy(h):
        return pltpu.make_async_copy(acts.at[h], slot(h, along, across, core), own_sem.at[h])

    for h in range(halves):
        total = row_sum(h, 0)
        for d in order:
            z_copy(h, d).wait_recv()
            total = total + zland[h, d - 1].astype(jnp.float32)
        gate, up, grad = total[0], total[1], total[2]
        sig = jax.nn.sigmoid(gate)
        acts[h, 0] = (gate * sig * up).astype(jnp.bfloat16)
        acts[h, 1] = (grad * up * sig * (1.0 + gate * (1.0 - sig))).astype(jnp.bfloat16)
        acts[h, 2] = (grad * gate * sig).astype(jnp.bfloat16)
        src = acts.at[h]
        pass_on(h, along, across, True, True, src)
        spread(h, along, src)
        hand_copy(h, along, across, core, src).start()
        own_copy(h).start()

    for h in range(halves):
        if h % 2 == 1:
            for s in range(1, wide):
                take(h, along, column(s))
                pass_on(h, along, column(s), True, True)
                hand_copy(h, along, column(s), core).start()
    for far in range(1, tall):
        for h in range(halves):
            for s in range(wide if h % 2 == 1 else 1):
                for sign in (-1, 1):

                    @pl.when(along >= far if sign < 0 else along + far < tall)
                    def _(h=h, s=s, sign=sign):
                        i = along + sign * far
                        take(h, i, column(s))
                        pass_on(h, i, column(s), sign < 0, sign > 0)
                        if h % 2 == 0:
                            spread(h, i)
                        hand_copy(h, i, column(s), core).start()

    for h in range(0, halves, 2):
        for s in range(1, wide):
            for d in [0] + list(range(1, tall)):
                take(h, line(d), column(s))
                hand_copy(h, line(d), column(s), core).start()

    for h in range(halves):
        own_copy(h).wait()

        def finish(owner, carry, h=h):
            i, j = owner // wide, lax.rem(owner, wide)
            hand_copy(h, i, j, 1 - core).wait_recv()
            hand_copy(h, i, j, core).wait_send()
            mine = jnp.bool_(True) if h % 2 == 1 else j == across

            @pl.when(jnp.logical_and(mine, jnp.logical_and(i <= along, along < tall - 1)))
            def _():
                z_route(h, i, j, along + 1, up_send).wait_send()

            @pl.when(jnp.logical_and(mine, jnp.logical_and(i >= along, along > 0)))
            def _():
                z_route(h, i, j, along - 1, down_send).wait_send()

            return carry

        lax.fori_loop(0, chips, finish, 0)
        for s in range(1, wide):
            if h % 2 == 1:
                x_route(h, along, s).wait_send()
            else:
                for i in range(tall):
                    x_route(h, i, s).wait_send()
        for d in range(tall):
            for s in range(wide):
                pair_copy(h, s, d).wait_send()
                if s > 0:
                    x_copy(h, s, d).wait_send()
            if d > 0:
                z_copy(h, d).wait_send()


def exchange(parts, collective_id):
    count = lax.axis_size("seq")
    chips = count // 2
    tall = 4 if chips % 4 == 0 else chips
    wide = chips // tall
    inputs = len(parts)
    own = parts[0].shape[1] // count
    subs = 2 if inputs == 1 and own % 32 == 0 else 1
    halves = inputs * subs
    piece = own // subs
    shape = (3, 2, subs, wide, tall, piece, BLK)
    chunk = (3, piece, BLK)
    dma = pltpu.SemaphoreType.DMA
    anywhere = pl.BlockSpec(memory_space=pl.ANY)
    out = pl.pallas_call(
        functools.partial(exchange_kernel, count, inputs),
        out_shape=jax.ShapeDtypeStruct((inputs,) + shape, jnp.bfloat16),
        in_specs=[anywhere] * inputs,
        out_specs=anywhere,
        scratch_shapes=[
            pltpu.VMEM((halves, wide, tall) + chunk, jnp.float32),
            pltpu.VMEM((halves, wide, tall) + chunk, jnp.float32),
            pltpu.VMEM((halves, max(wide - 1, 1), tall) + chunk, jnp.bfloat16),
            pltpu.VMEM((halves, max(wide - 1, 1), tall) + chunk, jnp.bfloat16),
            pltpu.VMEM((halves, max(tall - 1, 1)) + chunk, jnp.bfloat16),
            pltpu.VMEM((halves, max(tall - 1, 1)) + chunk, jnp.bfloat16),
            pltpu.VMEM((halves,) + chunk, jnp.bfloat16),
            dma((halves, wide, tall)),
            dma((halves, wide, tall)),
            dma((halves, wide, tall)),
            dma((halves, wide, tall)),
            dma((halves, wide, tall)),
            dma((halves, tall)),
            dma((halves, tall)),
            dma((halves, chips)),
            dma((halves, chips)),
            dma((halves, wide, tall)),
            dma((halves, chips)),
            dma((halves, chips)),
            dma((halves, chips)),
            dma((halves,)),
        ],
        compiler_params=pltpu.CompilerParams(
            collective_id=collective_id, has_side_effects=True, vmem_limit_bytes=COMM_LIMIT
        ),
    )(*(part.reshape(shape) for part in parts))
    return out.reshape((inputs,) + parts[0].shape)


def rows_out_kernel(group, table_ref, act_ref, *refs):
    gates, ups, downs = refs[:group], refs[group : 2 * group], refs[2 * group : 3 * group]
    out_ref = refs[3 * group]
    step = pl.program_id(1)

    @pl.when(step == 0)
    def _():
        out_ref[...] = jnp.zeros_like(out_ref)

    out = jnp.zeros(out_ref.shape[2:], jnp.float32)
    grad = jnp.zeros(out_ref.shape[2:], jnp.float32)
    across = (((1,), (1,)), ((), ()))
    for at in range(group):
        rows = slice(at * ROWBLK, (at + 1) * ROWBLK)
        out += jnp.dot(act_ref[0, 0, rows, :], downs[at][...], preferred_element_type=jnp.float32)
        grad += lax.dot_general(
            jnp.concatenate([act_ref[0, 1, rows, :], act_ref[0, 2, rows, :]], axis=1),
            jnp.concatenate([gates[at][...], ups[at][...]], axis=1),
            across,
            preferred_element_type=jnp.float32,
        )
    out_ref[0, 0] += out
    out_ref[0, 1] += grad


def rows_out(table, first, row_blocks, capacity, acts, gate_w, up_w, down_w):
    feats = gate_w.shape[0]
    group = group_of(capacity)
    steps = capacity // group
    if acts.shape[0] == row_blocks:
        place = lambda row, step, table: (row, 0, step, 0)
    else:
        place = lambda row, step, table: (0, 0, row * steps + step, 0)
    flops = 6 * row_blocks * ROWBLK * feats * capacity * BLK
    return pl.pallas_call(
        functools.partial(rows_out_kernel, group),
        out_shape=jax.ShapeDtypeStruct((row_blocks, 2, ROWBLK, feats), jnp.float32),
        grid_spec=pltpu.PrefetchScalarGridSpec(
            num_scalar_prefetch=1,
            grid=(row_blocks, steps),
            in_specs=[pl.BlockSpec((1, 3, group * ROWBLK, BLK), place)]
            + weight_specs(first, group, feats),
            out_specs=pl.BlockSpec((1, 2, ROWBLK, feats), lambda row, step, table: (row, 0, 0, 0)),
        ),
        compiler_params=pltpu.CompilerParams(vmem_limit_bytes=PLAIN_LIMIT),
        cost_estimate=pl.CostEstimate(
            flops=flops, bytes_accessed=flops // ROWBLK, transcendentals=0
        ),
    )(table, acts, *([gate_w] * group + [up_w] * group + [down_w] * group))


def weights_out_kernel(first, capacity, scale, pieces, group, passing, table_ref, *refs):
    toks, cots, refs = refs[:pieces], refs[pieces : 2 * pieces], refs[2 * pieces :]
    flipped, cot_all, dense = refs[-3:]
    units, refs = refs[:-3], None
    passed = ()
    if passing:
        units, passed = units[:-2], units[-2:]
    gate_ref, up_ref, down_ref = units[-3:]
    units = units[:-3]
    step = pl.program_id(0)
    rows = flipped.shape[1]
    row_blocks = rows // ROWBLK
    each = rows // pieces

    @pl.when(step == 0)
    def _():
        for at in range(pieces):
            cut = slice(at * each, (at + 1) * each)
            flipped[:, cut] = toks[at][...].T
            cot_all[cut, :] = cots[at][...]
        for at, out in enumerate(passed):
            out[...] = units[-1][at]

    act_ref = units[0]
    held = act_ref.shape[2] // ROWBLK
    for at in range(group):
        for row in range(row_blocks):
            unit = table_ref[first + row, capacity + 1 + step * group + at]
            index = jnp.maximum(unit, 0) + row * capacity
            lead, index = index // held, lax.rem(index, held)
            taken = pl.ds(pl.multiple_of(index * ROWBLK, ROWBLK), ROWBLK)
            for which in range(3):
                value = act_ref[lead, which, taken, :]
                dense[which, row * ROWBLK : (row + 1) * ROWBLK, at * BLK : (at + 1) * BLK] = (
                    jnp.where(unit >= 0, value, jnp.zeros_like(value))
                )
    tok = flipped[...]
    gate_ref[...] = jnp.dot(tok, dense[1], preferred_element_type=jnp.float32) * scale
    up_ref[...] = jnp.dot(tok, dense[2], preferred_element_type=jnp.float32) * scale
    down_ref[...] = (
        lax.dot_general(
            dense[0], cot_all[...], (((0,), (0,)), ((), ())), preferred_element_type=jnp.float32
        )
        * scale
    )


def weights_out(table, first, capacity, toks, cots, acts, scale, passing=None):
    blocks = table.shape[1] - capacity - 1
    feats = toks[0].shape[1]
    pieces = len(toks)
    rows = pieces * toks[0].shape[0]
    group = wide_group(blocks)
    whole = pl.BlockSpec(toks[0].shape, lambda step, table: (0, 0))
    wide = pl.BlockSpec((feats, group * BLK), lambda step, table: (0, step))
    hidden = blocks * BLK

    extra, extra_shapes, extra_in = (), (), []
    if passing is not None:
        extra = (passing,)
        extra_shapes = (jax.ShapeDtypeStruct(passing.shape[1:], passing.dtype),) * 2
        extra_in = [pl.BlockSpec(passing.shape, lambda step, table: (0, 0, 0))]

    return pl.pallas_call(
        functools.partial(
            weights_out_kernel, first, capacity, scale, pieces, group, passing is not None
        ),
        out_shape=(
            jax.ShapeDtypeStruct((feats, hidden), jnp.float32),
            jax.ShapeDtypeStruct((feats, hidden), jnp.float32),
            jax.ShapeDtypeStruct((hidden, feats), jnp.float32),
        )
        + extra_shapes,
        grid_spec=pltpu.PrefetchScalarGridSpec(
            num_scalar_prefetch=1,
            grid=(blocks // group,),
            in_specs=[whole] * (2 * pieces)
            + [pl.BlockSpec(acts.shape, lambda step, table: (0, 0, 0, 0))]
            + extra_in,
            out_specs=(
                wide,
                wide,
                pl.BlockSpec((group * BLK, feats), lambda step, table: (step, 0)),
            )
            + (whole,) * len(extra_shapes),
            scratch_shapes=[
                pltpu.VMEM((feats, rows), jnp.bfloat16),
                pltpu.VMEM((rows, feats), jnp.bfloat16),
                pltpu.VMEM((3, rows, group * BLK), jnp.bfloat16),
            ],
        ),
        compiler_params=pltpu.CompilerParams(vmem_limit_bytes=WIDE_LIMIT),
        cost_estimate=pl.CostEstimate(
            flops=6 * rows * feats * hidden, bytes_accessed=12 * feats * hidden, transcendentals=0
        ),
    )(table, *toks, *cots, acts, *extra)


def fused_kernel(mode, count, *refs):
    swapped, both = mode == "other", mode == "both"
    rows_held = 2 if both else 1
    moving = swapped or both
    table_ref, tok_ref, cot_ref, gate_hbm, up_hbm, down_hbm = refs[:6]
    refs = refs[6:]
    acts_out, tok_out, cot_out = refs[:3] if moving else (refs[0], None, None)
    refs = refs[3 if moving else 1 :]
    outs, refs = refs[:rows_held], refs[rows_held:]
    (
        gate_w, up_w, down_w, toks, cots, parts, paired, xsend, xland, zsend, zland, acts,
        sums, weight_sem, row_load, row_send, row_recv, row_store, pair_send, pair_recv, x_send, x_recv,
        z_send, z_recv, up_send, down_send, side_send, all_recv, hand_send, hand_recv, out_sem,
    ) = refs
    groups, _, held, _ = parts.shape
    rows = toks.shape[0]
    first = 1 if swapped else 0
    units = held // ROWBLK
    _, wide, tall, _, piece, _ = paired.shape
    chips = count // 2
    me, rank = lax.axis_index("seq"), lax.axis_index("tp")
    chip, core = me // 2, lax.rem(me, 2)
    sibling, partner = {"seq": me + 1 - 2 * core}, {"tp": 1 - rank}
    along, across = chip // wide, lax.rem(chip, wide)
    order = sorted(range(1, tall), key=lambda shift: abs(2 * shift - tall))
    contract = (((1,), (1,)), ((), ()))

    def device(i, j):
        return {"seq": (i * wide + j) * 2 + core}

    def column(shift):
        return lax.rem(across + shift, wide)

    def line(shift):
        return lax.rem(along + shift, tall)

    def rows_of(side, i, j):
        return pl.ds(pl.multiple_of(((side * wide + j) * tall + i) * piece, 16), piece)

    def remote(src, dst, send, recv, target):
        return pltpu.make_async_remote_copy(
            src_ref=src, dst_ref=dst, send_sem=send, recv_sem=recv,
            device_id=target, device_id_type=MESH,
        )

    def signal(target):
        pl.semaphore_signal(
            pltpu.get_barrier_semaphore(), inc=1, device_id=target, device_id_type=MESH
        )

    blocks = down_w.shape[0]
    own_rows = [
        pltpu.make_async_copy(src, dst.at[0], row_load.at[at])
        for at, (src, dst) in enumerate(((tok_ref, toks), (cot_ref, cots)))
        if not swapped
    ]

    def start_columns(block, carry):
        cut = pl.ds(pl.multiple_of(block * BLK, BLK), BLK)
        pltpu.make_async_copy(gate_hbm.at[:, cut], gate_w.at[block], weight_sem.at[0]).start()
        pltpu.make_async_copy(up_hbm.at[:, cut], up_w.at[block], weight_sem.at[1]).start()
        return carry

    def start_lines(block, carry):
        cut = pl.ds(pl.multiple_of(block * BLK, BLK), BLK)
        pltpu.make_async_copy(down_hbm.at[cut, :], down_w.at[block], weight_sem.at[2]).start()
        return carry

    for copy in own_rows:
        copy.start()
    lax.fori_loop(0, blocks, start_columns, 0)
    lax.fori_loop(0, blocks, start_lines, 0)

    signal(sibling)
    for s in range(1, wide):
        signal(device(along, column(s)))
    for d in range(1, tall):
        signal(device(line(d), across))
    if moving:
        signal(partner)
    pl.semaphore_wait(pltpu.get_barrier_semaphore(), wide + tall - 1 + (1 if moving else 0))

    row_copies = [
        remote(src, dst.at[rows - 1], row_send.at[at], row_recv.at[at], partner)
        for at, (src, dst) in enumerate(((tok_ref, toks), (cot_ref, cots)))
        if moving
    ]
    for copy in row_copies:
        copy.start()
    row_stores = [
        pltpu.make_async_copy(src.at[rows - 1], dst, row_store.at[at])
        for at, (src, dst) in enumerate(((toks, tok_out), (cots, cot_out)))
        if moving
    ]

    def pair_copy(h, s, d):
        return remote(
            parts.at[h, :, rows_of(1 - core, line(d), column(s))], paired.at[h, s, d],
            pair_send.at[h, s, d], pair_recv.at[h, s, d], sibling,
        )

    def x_copy(h, s, d):
        return remote(
            xsend.at[h, s - 1, d], xland.at[h, s - 1, d],
            x_send.at[h, s, d], x_recv.at[h, s, d], device(along, column(s)),
        )

    def z_copy(h, d):
        return remote(
            zsend.at[h, d - 1], zland.at[h, d - 1],
            z_send.at[h, d], z_recv.at[h, d], device(line(d), across),
        )

    def slot(h, i, j, side):
        return acts.at[h, :, rows_of(side, i, j)]

    def z_route(h, i, j, to, send):
        dst, owner = slot(h, i, j, core), i * wide + j
        return remote(
            dst, dst, send.at[h, owner], all_recv.at[h, owner], device(to, across)
        )

    def x_route(h, i, s):
        dst = slot(h, i, across, core)
        return remote(
            dst, dst, side_send.at[h, s, i], all_recv.at[h, i * wide + across],
            device(along, column(s)),
        )

    def hand_copy(h, i, j, side):
        dst, owner = slot(h, i, j, side), i * wide + j
        return remote(dst, dst, hand_send.at[h, owner], hand_recv.at[h, owner], sibling)

    def out_copy(h):
        return pltpu.make_async_copy(acts.at[h], acts_out.at[h], out_sem.at[h])

    def take(h, i, j):
        z_route(h, i, j, along, up_send).wait_recv()

    def pass_on(h, i, j, up, down):
        if up:

            @pl.when(along < tall - 1)
            def _():
                z_route(h, i, j, along + 1, up_send).start()

        if down:

            @pl.when(along > 0)
            def _():
                z_route(h, i, j, along - 1, down_send).start()

    def spread(h, i):
        for s in range(1, wide):
            x_route(h, i, s).start()

    def line_first(h):
        return True

    def row_of(h):
        return h * rows // groups

    def block_of(h, unit):
        base = h % (groups // rows) * units
        return table_ref[first + row_of(h), base + unit]

    def unit_rows(unit):
        return pl.ds(pl.multiple_of(unit * ROWBLK, ROWBLK), ROWBLK)

    begin = (1 - core) * (units // 2 // 2)

    def column_step(h, pair):
        tok = toks[row_of(h)]
        for one in range(2):
            block, at = block_of(h, 2 * pair + one), unit_rows(2 * pair + one)
            value = jnp.dot(
                tok,
                jnp.concatenate([gate_w[block], up_w[block]], axis=1),
                preferred_element_type=jnp.float32,
            )
            parts[h, 0, at, :] = value[:, :BLK]
            parts[h, 1, at, :] = value[:, BLK:]

    def line_step(h, pair):
        grad = lax.dot_general(
            cots[row_of(h)],
            jnp.concatenate(
                [down_w[block_of(h, 2 * pair)], down_w[block_of(h, 2 * pair + 1)]], axis=0
            ),
            contract,
            preferred_element_type=jnp.float32,
        )
        parts[h, 2, unit_rows(2 * pair), :] = grad[:, :BLK]
        parts[h, 2, unit_rows(2 * pair + 1), :] = grad[:, BLK:]

    def each_pair(h, low, high, *steps):
        def body(turn, carry):
            for step in steps:
                step(h, lax.rem(turn + begin, units // 2))
            return carry

        lax.fori_loop(low, high, body, 0)

    def columns_times(h, low, high):
        each_pair(h, low, high, column_step)

    def lines_times(h, low, high):
        each_pair(h, low, high, line_step)

    def multiply(h, low, high):
        each_pair(h, low, high, column_step, line_step)

    def pair_stage(h):
        for s in list(range(1, wide)) + [0]:
            for d in order + [0]:
                pair_copy(h, s, d).start()

    def x_stage(h):
        for d in order + [0]:
            for s in range(1, wide):
                pair_copy(h, s, d).wait_recv()
                xsend[h, s - 1, d] = (
                    parts[h, :, rows_of(core, line(d), column(s)), :] + paired[h, s, d]
                ).astype(jnp.bfloat16)
                x_copy(h, s, d).start()

    def row_sum(h, d):
        pair_copy(h, 0, d).wait_recv()
        total = parts[h, :, rows_of(core, line(d), across), :] + paired[h, 0, d]
        for s in range(1, wide):
            x_copy(h, s, d).wait_recv()
            total = total + xland[h, s - 1, d].astype(jnp.float32)
        return total

    def z_piece(h, at):
        d = order[at]
        zsend[h, d - 1] = row_sum(h, d).astype(jnp.bfloat16)
        z_copy(h, d).start()

    def z_stage(h):
        for at in range(len(order)):
            z_piece(h, at)

    def act_stage(h):
        total = row_sum(h, 0)
        for d in order:
            z_copy(h, d).wait_recv()
            total = total + zland[h, d - 1].astype(jnp.float32)
        gate, up, grad = total[0], total[1], total[2]
        sig = jax.nn.sigmoid(gate)
        own = rows_of(core, along, across)
        acts[h, 0, own, :] = (gate * sig * up).astype(jnp.bfloat16)
        acts[h, 1, own, :] = (grad * up * sig * (1.0 + gate * (1.0 - sig))).astype(jnp.bfloat16)
        acts[h, 2, own, :] = (grad * gate * sig).astype(jnp.bfloat16)
        pass_on(h, along, across, True, True)
        spread(h, along)
        hand_copy(h, along, across, core).start()

    def gather_stage(h, far):
        if far == 1 and not line_first(h):
            for s in range(1, wide):
                take(h, along, column(s))
                pass_on(h, along, column(s), True, True)
                hand_copy(h, along, column(s), core).start()
        for s in range(1 if line_first(h) else wide):
            for sign in (-1, 1):

                @pl.when(along >= far if sign < 0 else along + far < tall)
                def _(s=s, sign=sign):
                    i = along + sign * far
                    take(h, i, column(s))
                    pass_on(h, i, column(s), sign < 0, sign > 0)
                    if line_first(h):
                        spread(h, i)
                    hand_copy(h, i, column(s), core).start()

    def side_stage(h):
        if line_first(h):
            for s in range(1, wide):
                for d in range(tall):
                    take(h, line(d), column(s))
                    hand_copy(h, line(d), column(s), core).start()

    def sums_stage(h):
        def arrive(owner, carry):
            hand_copy(h, owner // wide, lax.rem(owner, wide), 1 - core).wait_recv()
            return carry

        lax.fori_loop(0, chips, arrive, 0)
        out_copy(h).start()
        row = row_of(h)

        def step(pair, carry):
            at = (unit_rows(2 * pair), unit_rows(2 * pair + 1))
            cut = (block_of(h, 2 * pair), block_of(h, 2 * pair + 1))
            sums[row, 0] += jnp.dot(
                jnp.concatenate([acts[h, 0, at[0], :], acts[h, 0, at[1], :]], axis=1),
                jnp.concatenate([down_w[cut[0]], down_w[cut[1]]], axis=0),
                preferred_element_type=jnp.float32,
            )
            grad = sums[row, 1]
            for one in range(2):
                grad += lax.dot_general(
                    jnp.concatenate([acts[h, 1, at[one], :], acts[h, 2, at[one], :]], axis=1),
                    jnp.concatenate([gate_w[cut[one]], up_w[cut[one]]], axis=1),
                    contract,
                    preferred_element_type=jnp.float32,
                )
            sums[row, 1] = grad
            return carry

        lax.fori_loop(0, units // 2, step, 0)

    sums[...] = jnp.zeros_like(sums)
    for copy in own_rows:
        copy.wait()
    half = (units // 2 + 1) // 2

    def weights_arrive(at, held_w):
        pltpu.make_async_copy(held_w, held_w, weight_sem.at[at]).wait()

    pairs = units // 2
    early = groups > 2
    for h in range(groups):
        crossing = moving and h == (0 if swapped else groups // 2)
        if h == 0:
            weights_arrive(0, gate_w)
            weights_arrive(1, up_w)
        if crossing:
            row_copies[0].wait_recv()
        columns_times(h, 0, half)
        if h == 0:
            weights_arrive(2, down_w)
        if crossing:
            row_copies[1].wait_recv()
            for copy in row_stores:
                copy.start()
        lines_times(h, 0, half)
        pair_stage(h)
        multiply(h, half, pairs)
        if h > 0:
            for at in range(len(order) - 1):
                z_piece(h - 1, at)
        x_stage(h)
        if h > 0:
            z_piece(h - 1, len(order) - 1)
        if early and h == groups - 1:
            act_stage(0)
    last = tall + 1
    for turn in range(groups + last):
        if turn == groups - 2:
            z_stage(groups - 1)
        if 0 <= turn - last < groups:
            sums_stage(turn - last)
        for h in range(groups):
            at = turn - h
            if 1 <= at < tall:
                gather_stage(h, at)
            elif at == tall:
                side_stage(h)
            elif at == 0 and not (early and h == 0):
                act_stage(h)

    alive = table_ref[first + rows - 1, table_ref.shape[1] - 1].astype(jnp.float32)
    for row, out in enumerate(outs):
        value = sums[row]
        if both:
            value = value * alive
        out[...] = value.astype(out.dtype)

    for h in range(groups):

        def finish(owner, carry, h=h):
            i, j = owner // wide, lax.rem(owner, wide)
            hand_copy(h, i, j, core).wait_send()
            mine = j == across if line_first(h) else jnp.bool_(True)

            @pl.when(jnp.logical_and(mine, jnp.logical_and(i <= along, along < tall - 1)))
            def _():
                z_route(h, i, j, along + 1, up_send).wait_send()

            @pl.when(jnp.logical_and(mine, jnp.logical_and(i >= along, along > 0)))
            def _():
                z_route(h, i, j, along - 1, down_send).wait_send()

            return carry

        lax.fori_loop(0, chips, finish, 0)
        for s in range(1, wide):
            if line_first(h):
                for i in range(tall):
                    x_route(h, i, s).wait_send()
            else:
                x_route(h, along, s).wait_send()
        for d in range(tall):
            for s in range(wide):
                pair_copy(h, s, d).wait_send()
                if s > 0:
                    x_copy(h, s, d).wait_send()
            if d > 0:
                z_copy(h, d).wait_send()
        out_copy(h).wait()
    for copy in row_copies:
        copy.wait_send()
    for copy in row_stores:
        copy.wait()


def fused(mode, table, capacity, tok, cot, gate_w, up_w, down_w, collective_id):
    count = lax.axis_size("seq")
    chips = count // 2
    tall = 4 if chips % 4 == 0 else chips
    wide = chips // tall
    rows = 2 if mode == "both" else 1
    groups = 2 * rows
    feats, blocks = gate_w.shape[0], gate_w.shape[1] // BLK
    held = capacity // 2 * ROWBLK
    piece = held // count
    chunk = (3, piece, BLK)
    dma = pltpu.SemaphoreType.DMA
    anywhere = pl.BlockSpec(memory_space=pl.ANY)
    out_shape = [jax.ShapeDtypeStruct((groups, 3, held, BLK), jnp.bfloat16)]
    out_specs = [anywhere]
    if mode != "own":
        out_shape += [jax.ShapeDtypeStruct(tok.shape, tok.dtype)] * 2
        out_specs += [anywhere] * 2
    if mode == "both":
        out_shape += [jax.ShapeDtypeStruct((2,) + tok.shape, jnp.float32)]
    out_shape += [jax.ShapeDtypeStruct((2,) + tok.shape, jnp.bfloat16)]
    out_specs += [pl.BlockSpec(memory_space=pltpu.VMEM)] * rows
    flops = 12 * rows * ROWBLK * tok.shape[1] * capacity * BLK
    return pl.pallas_call(
        functools.partial(fused_kernel, mode, count),
        out_shape=tuple(out_shape),
        in_specs=[pl.BlockSpec(memory_space=pltpu.SMEM)] + [anywhere] * 5,
        out_specs=tuple(out_specs),
        scratch_shapes=[
            pltpu.VMEM((blocks, feats, BLK), gate_w.dtype),
            pltpu.VMEM((blocks, feats, BLK), up_w.dtype),
            pltpu.VMEM((blocks, BLK, feats), down_w.dtype),
            pltpu.VMEM((rows,) + tok.shape, tok.dtype),
            pltpu.VMEM((rows,) + tok.shape, tok.dtype),
            pltpu.VMEM((groups, 3, held, BLK), jnp.float32),
            pltpu.VMEM((groups, wide, tall) + chunk, jnp.float32),
            pltpu.VMEM((groups, wide - 1, tall) + chunk, jnp.bfloat16),
            pltpu.VMEM((groups, wide - 1, tall) + chunk, jnp.bfloat16),
            pltpu.VMEM((groups, tall - 1) + chunk, jnp.bfloat16),
            pltpu.VMEM((groups, tall - 1) + chunk, jnp.bfloat16),
            pltpu.VMEM((groups, 3, held, BLK), jnp.bfloat16),
            pltpu.VMEM((rows, 2) + tok.shape, jnp.float32),
            dma((3,)),
            dma((2,)),
            dma((2,)),
            dma((2,)),
            dma((2,)),
            dma((groups, wide, tall)),
            dma((groups, wide, tall)),
            dma((groups, wide, tall)),
            dma((groups, wide, tall)),
            dma((groups, tall)),
            dma((groups, tall)),
            dma((groups, chips)),
            dma((groups, chips)),
            dma((groups, wide, tall)),
            dma((groups, chips)),
            dma((groups, chips)),
            dma((groups, chips)),
            dma((groups,)),
        ],
        compiler_params=pltpu.CompilerParams(
            collective_id=collective_id, has_side_effects=True, vmem_limit_bytes=FUSED_LIMIT
        ),
        cost_estimate=pl.CostEstimate(
            flops=flops, bytes_accessed=6 * gate_w.size, transcendentals=0
        ),
    )(table, tok, cot, gate_w, up_w, down_w)


def shards(tokens, gate_weight, up_weight, down_weight, masks, cotangent):
    tp_count = lax.axis_size("tp")
    seq_count = lax.axis_size("seq")
    rank = lax.axis_index("tp")
    rows, feats = tokens.shape
    total_rows = rows * tp_count
    row_blocks, blocks = masks.shape
    kept_total = blocks * tp_count // KEEP_PART
    capacity = min(2 * kept_total // tp_count, blocks)
    scale = 1.0 / math.sqrt(total_rows)
    weights = (gate_weight, up_weight, down_weight)

    fits = seq_count % 8 == 0 and capacity % 4 == 0 and capacity // 2 * ROWBLK % (16 * seq_count) == 0
    if tp_count != 2 or row_blocks != 2 or rows != ROWBLK or not fits:
        table, _, _ = unit_tables(masks, jnp.int32(0), capacity)
        tok, cot = (value.reshape(total_rows, feats) for value in gather_rows(tokens, cotangent))
        parts = partial_products(table, 0, capacity, tok, cot, *weights)
        acts = exchange([parts], 1)
        row_parts = rows_out(table, 0, row_blocks, capacity, acts, *weights)
        row_parts = jnp.swapaxes(row_parts.reshape(tp_count, rows // ROWBLK, 2, ROWBLK, feats), 1, 2)
        moved = []
        for shift in range(1, tp_count):
            piece = lax.dynamic_index_in_dim(
                row_parts, lax.rem(rank + shift, tp_count), 0, keepdims=False
            ).astype(jnp.bfloat16)
            pairs = [(src, (src + shift) % tp_count) for src in range(tp_count)]
            moved.append(lax.ppermute(piece, "tp", pairs))
        grads = weights_out(table, 0, capacity, [tok], [cot], acts, scale)
        mine = lax.dynamic_index_in_dim(row_parts, rank, 0, keepdims=False)
        for piece in moved:
            mine = mine + piece.astype(jnp.float32)
        mine = mine.reshape(2, rows, feats).astype(jnp.bfloat16)
        return (mine[0], mine[1]) + tuple(grads)

    table, index, case = unit_tables(masks, rank, capacity)

    def swap(value):
        return lax.ppermute(value, "tp", [(0, 1), (1, 0)])

    def one_row(own, _):
        first = 0 if own else 1
        acts, *rest = fused(
            "own" if own else "other", index, capacity, tokens, cotangent, *weights, 2 + first
        )
        if own:
            grads = weights_out(table, 0, capacity, [tokens], [cotangent], acts, scale, rest[0])
            return tuple(grads[3:]) + tuple(grads[:3])
        tok, cot, sums = rest
        sums = swap(sums)
        grads = weights_out(table, 1, capacity, [tok], [cot], acts, scale)
        return (sums[0], sums[1]) + tuple(grads)

    def both_rows(_):
        acts, tok, cot, mine, other = fused(
            "both", index, capacity, tokens, cotangent, *weights, 1
        )
        moved = swap(other)
        grads = weights_out(table, 0, capacity, [tokens, tok], [cotangent, cot], acts, scale)
        total = (mine + moved.astype(jnp.float32)).astype(jnp.bfloat16)
        return (total[0], total[1]) + tuple(grads)

    return lax.switch(
        case[0],
        [functools.partial(one_row, True), functools.partial(one_row, False), both_rows],
        None,
    )


def solution(mesh):
    placed = (
        P("tp", "seq"),
        P("seq", "tp"),
        P("seq", "tp"),
        P("tp", "seq"),
        P(None, "tp"),
        P("tp", "seq"),
    )
    return jax.shard_map(
        shards,
        mesh=mesh,
        in_specs=placed,
        out_specs=(P("tp", "seq"), P("tp", "seq"), P("seq", "tp"), P("seq", "tp"), P("tp", "seq")),
        check_vma=False,
    )
```
